256 devices in a mesh: req: 32 (over z, x), tp: 8 (over y, core).
Axes of the slice: x: 4, y: 4, z: 8, core: 2. Of those that a mesh axis runs over, the one named last changes fastest.
Arguments:
- hidden_in: bfloat16 [192, 64, 3072], P('req', None, 'tp'), may hold values from -3 to 3
- request_order: int32 [192], replicated, may hold values from 0 to 191, as said below
- norm_gain: bfloat16 [3072], replicated, may hold values from 0.099609375 to 1.8984375
- w_query: bfloat16 [3072, 3072], P(None, 'tp'), may hold values from -0.109375 to 0.109375
- key_weight: bfloat16 [3072, 1024], P(None, 'tp'), may hold values from -0.4375 to 0.4375
- value_weight: bfloat16 [3072, 1024], P(None, 'tp'), may hold values from -0.109375 to 0.109375
- w_out: bfloat16 [3072, 3072], P('tp'), may hold values from -0.109375 to 0.109375
- key_cache: bfloat16 [192, 8, 3456, 128], P('req', 'tp'), may hold values from -360 to 360
- cached_values: bfloat16 [192, 8, 3456, 128], P('req', 'tp'), may hold values from -24 to 24
- cache_lengths: int32 [192], P('req'), may hold values from 864 to 3456, as said below
- tree_parent: int32 [192, 64], P('req'), may hold values from 0 to 63, as said below
- kept_nodes: int32 [192, 8], P('req'), may hold values from 0 to 63
Outputs:
- layer_out: bfloat16 [192, 64, 3072], P('req', None, 'tp')
- appended: bfloat16 [192, 2, 8, 8, 128], P('req', None, None, 'tp')
The draws below stay inside these ranges and needn't reach their ends.
Inputs may be any that keep to these rules, and one draw needn't show every extreme that they name: `request_order`: each request is held by exactly one slot. The 6 requests of one device's rows go to 6 different devices of req, and the slots of one device hold requests of 6 different devices. `cache_lengths`: some slot has exactly 3456 live positions. `tree_parent`: node 0 has parent 0; every other node's parent has a lower index.
All inputs are finite; a program needn't handle non-finite values.
Results may differ from the reference program's by a relative error of at most 0.0085.
The reference program's roundings to bfloat16 on the way count: a program that leaves them out, or rounds other values in their place, can miss the bound.
Values may be sent and summed in bfloat16 or wider, within the bound.
A program may use at most 128 MiB of HBM per device.

```python
import jax
import jax.numpy as jnp
from jax import lax

MODEL_WIDTH = 3072
QUERY_HEADS = 24
KEY_VALUE_HEADS = 8
HEAD_WIDTH = 128
R_DEV = 6
CACHE_CAPACITY = 3456
DRAFT = 64
KEEP = 8
REQUEST_COUNT = 192


def draw_request_order(key, part):
    groups = REQUEST_COUNT // R_DEV
    shuffled = jax.random.permutation(jax.random.fold_in(key, 11), groups).astype(jnp.int32)
    position = jnp.arange(groups, dtype=jnp.int32)
    priority = jnp.where(shuffled == groups // 2, 0, jnp.where(shuffled == 1, 1, position + 2))
    offsets = shuffled[jnp.argsort(priority, stable=True)][:R_DEV].astype(jnp.int32)
    row_perms = jax.vmap(lambda k: jax.random.permutation(k, R_DEV))(jax.random.split(jax.random.fold_in(key, 12), groups)).astype(jnp.int32)
    slot_perms = jax.vmap(lambda k: jax.random.permutation(k, R_DEV))(jax.random.split(jax.random.fold_in(key, 13), groups)).astype(jnp.int32)
    source = jnp.arange(groups, dtype=jnp.int32)[:, None]
    column = jnp.arange(R_DEV, dtype=jnp.int32)[None, :]
    target = (source + offsets[None, :]) % groups
    slots = target * R_DEV + slot_perms[target, jnp.broadcast_to(column, target.shape)]
    requests = source * R_DEV + row_perms
    order = jnp.zeros((REQUEST_COUNT,), jnp.int32).at[slots.reshape(-1)].set(requests.reshape(-1))
    return order


def draw_key_cache(key, part):
    rotary_base = jnp.clip(jax.random.normal(key, (REQUEST_COUNT, KEY_VALUE_HEADS, CACHE_CAPACITY, HEAD_WIDTH), jnp.float32), -6.0, 6.0)
    return rotary_base.astype(jnp.bfloat16)


def draw_cache_lengths(key, part):
    lengths = jax.random.randint(key, (REQUEST_COUNT,), CACHE_CAPACITY // 4, CACHE_CAPACITY + 1, dtype=jnp.int32)
    longest = jax.random.randint(jax.random.fold_in(key, 1), (), 0, REQUEST_COUNT, dtype=jnp.int32)
    return lengths.at[longest].set(CACHE_CAPACITY)


def draw_tree_parent(key, part):
    upper = jnp.maximum(jnp.arange(DRAFT, dtype=jnp.int32), 1)
    return jax.random.randint(key, (REQUEST_COUNT, DRAFT), 0, upper[None, :], dtype=jnp.int32)


def plant(array, key, least, top_value):
    spot = [jax.random.randint(jax.random.fold_in(key, axis), (), 0, length) for axis, length in enumerate(array.shape)]
    widest = array.shape.index(max(array.shape))
    beside = spot[:widest] + [(spot[widest] + 1) % array.shape[widest]] + spot[widest + 1:]
    return array.at[tuple(spot)].set(least).at[tuple(beside)].set(top_value)


def block_levels(rng, extent, pieces, low, high):
    level, own = 1.0, jax.random.fold_in(rng, 6)
    for dim, blocks in pieces:
        heights = jnp.exp(jax.random.uniform(jax.random.fold_in(own, dim), (blocks,), jnp.float32, low / len(pieces), high / len(pieces)))
        level = level * jnp.repeat(heights, extent[dim] // blocks).reshape([-1 if axis == dim else 1 for axis in range(len(extent))])
    return level


def normal_values(key, shape, scale, reach, cuts=(), held_as=jnp.bfloat16):
    level = block_levels(key, shape, cuts, -0.22, 0.18) if cuts else 1.0
    drawn = jax.random.normal(key, shape, jnp.float32) * scale * level
    return jnp.minimum(jnp.maximum(drawn, -reach), reach).astype(held_as)


def setup_inputs(seed: int = 0) -> dict:
    seeds = jax.random.split(jax.random.key(seed), 13)
    hidden_in = normal_values(seeds[0], (REQUEST_COUNT, DRAFT, MODEL_WIDTH), 0.5, 3.0, ((0, 32), (2, 8)))
    request_order = draw_request_order(jax.random.fold_in(seeds[12], 71), 0)
    norm_gain = jnp.clip(1.0 + 0.18 * jax.random.normal(seeds[2], (MODEL_WIDTH,), jnp.float32), 0.099609375, 1.8984375).astype(jnp.bfloat16)
    w_query = normal_values(seeds[3], (MODEL_WIDTH, QUERY_HEADS * HEAD_WIDTH), MODEL_WIDTH ** -0.5, 0.109375, ((1, 8),))
    key_weight = normal_values(seeds[4], (MODEL_WIDTH, KEY_VALUE_HEADS * HEAD_WIDTH), (MODEL_WIDTH // 16) ** -0.5, 0.4375, ((1, 8),))
    value_weight = normal_values(seeds[5], (MODEL_WIDTH, KEY_VALUE_HEADS * HEAD_WIDTH), MODEL_WIDTH ** -0.5, 0.109375, ((1, 8),))
    w_out = normal_values(seeds[6], (QUERY_HEADS * HEAD_WIDTH, MODEL_WIDTH), (QUERY_HEADS * HEAD_WIDTH) ** -0.5, 0.109375, ((0, 8),))
    key_cache = draw_key_cache(jax.random.fold_in(seeds[12], 71), 0)
    cached_values = normal_values(seeds[8], (REQUEST_COUNT, KEY_VALUE_HEADS, CACHE_CAPACITY, HEAD_WIDTH), 4.0, 24.0, ((0, 32), (1, 8)))
    cache_lengths = draw_cache_lengths(jax.random.fold_in(seeds[12], 71), 0)
    tree_parent = draw_tree_parent(jax.random.fold_in(seeds[12], 71), 0)
    kept_nodes = plant(jax.random.randint(seeds[11], (REQUEST_COUNT, KEEP), 0, DRAFT), jax.random.fold_in(seeds[11], 1), 0, DRAFT - 1).astype(jnp.int32)
    return {"hidden_in": hidden_in, "request_order": request_order, "norm_gain": norm_gain, "w_query": w_query, "key_weight": key_weight, "value_weight": value_weight, "w_out": w_out, "key_cache": key_cache, "cached_values": cached_values, "cache_lengths": cache_lengths, "tree_parent": tree_parent, "kept_nodes": kept_nodes}


NORM_EPSILON = 1e-05

def ancestors(parent_row):
    tree_length = parent_row.shape[0]
    node_ids = jnp.arange(tree_length, dtype=jnp.int32)
    parent_link = ((parent_row[:, None] == node_ids[None, :]) & (node_ids[:, None] > 0)).astype(jnp.float32)
    ancestry = jnp.eye(tree_length, dtype=jnp.float32) + parent_link
    for sweep in range(tree_length.bit_length()):
        ancestry = jnp.minimum(jnp.dot(ancestry, ancestry, precision=lax.Precision.HIGHEST), 1.0)
    return ancestry

def rotary_embedding(vectors, token_positions):
    half_dim = vectors.shape[-1] // 2
    frequency = 500000.0 ** (-jnp.arange(half_dim, dtype=jnp.float32) * 2.0 / vectors.shape[-1])
    angles = token_positions[..., None] * frequency
    cosine = jnp.cos(angles)[..., None, :]
    sine = jnp.sin(angles)[..., None, :]
    first_half = vectors[..., :half_dim]
    second_half = vectors[..., half_dim:]
    return jnp.concatenate([first_half * cosine - second_half * sine, second_half * cosine + first_half * sine], axis=-1)

def reference(hidden_in, request_order, norm_gain, w_query, key_weight, value_weight, w_out, key_cache, cached_values, cache_lengths, tree_parent, kept_nodes):
    dealt_all = hidden_in[request_order]
    group_width = QUERY_HEADS // KEY_VALUE_HEADS
    score_scale = HEAD_WIDTH ** (-0.5)

    def one_slot(items):
        dealt, keys_old, values_old, length, parent_row, kept_row = items
        tree_length = dealt.shape[0]
        widened = dealt.astype(jnp.float32)
        normalized_input = (widened * lax.rsqrt(lax.optimization_barrier(jnp.mean(widened * widened, axis=-1, keepdims=True)) + NORM_EPSILON) * norm_gain.astype(jnp.float32)).astype(jnp.bfloat16)
        query_rows = jnp.dot(normalized_input, w_query, preferred_element_type=jnp.float32).reshape(tree_length, QUERY_HEADS, HEAD_WIDTH)
        fresh_keys = jnp.dot(normalized_input, key_weight, preferred_element_type=jnp.float32).reshape(tree_length, KEY_VALUE_HEADS, HEAD_WIDTH)
        fresh_values = jnp.dot(normalized_input, value_weight, preferred_element_type=jnp.float32).astype(jnp.bfloat16).reshape(tree_length, KEY_VALUE_HEADS, HEAD_WIDTH)
        ancestry = ancestors(parent_row)
        token_positions = length.astype(jnp.float32) + lax.optimization_barrier(jnp.sum(ancestry, axis=-1)) - 1.0
        rotated_query = rotary_embedding(query_rows, token_positions).astype(jnp.bfloat16).reshape(tree_length, KEY_VALUE_HEADS, group_width, HEAD_WIDTH)
        key_rot = rotary_embedding(fresh_keys, token_positions).astype(jnp.bfloat16)
        cache_scores = jnp.einsum('tgqd,gcd->gqtc', rotated_query.astype(jnp.float32), keys_old.astype(jnp.float32)) * score_scale
        live_keys = jnp.arange(keys_old.shape[1], dtype=jnp.int32) < length
        cache_scores = jnp.where(live_keys[None, None, None, :], cache_scores, -jnp.inf)
        tree_scores = jnp.einsum('tgqd,sgd->gqts', rotated_query.astype(jnp.float32), key_rot.astype(jnp.float32)) * score_scale
        tree_scores = jnp.where(ancestry[None, None] > 0, tree_scores, -jnp.inf)
        row_max = jnp.maximum(lax.optimization_barrier(jnp.max(cache_scores, axis=-1)), lax.optimization_barrier(jnp.max(tree_scores, axis=-1)))
        cache_exp = jnp.exp(cache_scores - row_max[..., None])
        tree_exp = jnp.exp(tree_scores - row_max[..., None])
        row_total = lax.optimization_barrier(jnp.sum(cache_exp, axis=-1)) + lax.optimization_barrier(jnp.sum(tree_exp, axis=-1))
        cache_weights = (cache_exp / row_total[..., None]).astype(jnp.bfloat16)
        tree_weights = (tree_exp / row_total[..., None]).astype(jnp.bfloat16)
        attended = jnp.einsum('gqtc,gcd->tgqd', cache_weights.astype(jnp.float32), values_old.astype(jnp.float32))
        attended = attended + jnp.einsum('gqts,sgd->tgqd', tree_weights.astype(jnp.float32), fresh_values.astype(jnp.float32))
        attended = attended.astype(jnp.bfloat16).reshape(tree_length, QUERY_HEADS * HEAD_WIDTH)
        layer_out = (jnp.dot(attended, w_out, preferred_element_type=jnp.float32) + widened).astype(jnp.bfloat16)
        kept_keys = jnp.take(key_rot, kept_row, axis=0)
        kept_values = jnp.take(fresh_values, kept_row, axis=0)
        return (layer_out, jnp.stack([kept_keys, kept_values], axis=0))
    return lax.map(one_slot, (dealt_all, key_cache, cached_values, cache_lengths, tree_parent, kept_nodes))
```

```python
import functools
import math

import jax
import jax.numpy as jnp
import numpy as np
from jax import lax
from jax.experimental import pallas as pl
from jax.experimental.pallas import tpu as pltpu
from jax.sharding import PartitionSpec as P

MESH = pl.DeviceIdType.MESH
HEAD = 128
EPS = 1e-05
SLOTS, NODES, WIDTH = 6, 64, 384
NX, NZ, NY = 4, 8, 4
TP = 8
CACHE = 3456
KEEP = 8
CHUNKS = 4
ROWS = NODES // CHUNKS
BLOCK = 384
LOG2E = math.log2(math.e)
SCALE = HEAD ** (-0.5)


def remote(src, dst, send, recv, req, tp):
    return pltpu.make_async_remote_copy(
        src_ref=src, dst_ref=dst, send_sem=send, recv_sem=recv,
        device_id=(req, tp), device_id_type=MESH,
    )


def place():
    req = lax.axis_index("req")
    tp = lax.axis_index("tp")
    return req, tp, req // NX, req % NX, tp // 2, tp % 2


def greet(peers):
    barrier = pltpu.get_barrier_semaphore()
    for req, tp in peers:
        pl.semaphore_signal(barrier, inc=1, device_id=(req, tp), device_id_type=MESH)
    pl.semaphore_wait(barrier, len(peers))


def deal_kernel(order, hidden, full, *scratch):
    held = scratch[:CHUNKS]
    far_out, far_in, near_out, near_in = scratch[CHUNKS:CHUNKS + 4]
    (load_sem, z_send, z_recv, far_send, far_recv, near_send, near_recv,
     y_send, y_recv, half_send, half_recv, sib_send, sib_recv) = scratch[CHUNKS + 4:]
    req, tp, z, x, y, c = place()

    def at_z(step):
        return lax.rem(z + step + NZ, NZ) * NX + x

    def at_x(step):
        return z * NX + lax.rem(x + step + NX, NX)

    def at_y(step):
        return lax.rem(y + step + NY, NY) * 2 + c

    sign = (1, -1)
    sibling = y * 2 + 1 - c

    loads = [
        pltpu.make_async_copy(
            hidden.at[:, pl.ds(k * ROWS, ROWS), :], held[k].at[pl.ds(z * SLOTS, SLOTS)], load_sem.at[k]
        )
        for k in range(CHUNKS)
    ]
    for load in loads:
        load.start()
    greet([(at_z(1), tp), (at_z(-1), tp), (at_x(1), tp), (at_x(-1), tp),
           (req, at_y(1)), (req, at_y(-1)), (req, sibling)])

    def z_copy(k, hop, d, arriving):
        back = hop if arriving else hop - 1
        owner = lax.rem(z - sign[d] * back + 2 * NZ, NZ)
        count = SLOTS if hop < 4 else SLOTS // 2
        first = 0 if hop < 4 or d == 0 else SLOTS // 2
        block = held[k].at[pl.ds(owner * SLOTS + first, count)]
        return remote(block, block, z_send.at[d, hop - 1, k], z_recv.at[d, hop - 1, k], at_z(sign[d]), tp)

    def rows(k):
        return pl.ds(k * ROWS, ROWS)

    def far_copy(k, d):
        return remote(far_out.at[d, :, rows(k)], far_in.at[d, :, rows(k)],
                      far_send.at[d, k], far_recv.at[d, k], at_x(sign[d]), tp)

    def near_copy(k, d):
        return remote(near_out.at[d, :, rows(k)], near_in.at[d, :, rows(k)],
                      near_send.at[d, k], near_recv.at[d, k], at_x(sign[d]), tp)

    def y_copy(k, d, arriving):
        piece = full.at[at_y(-sign[d]) if arriving else tp, :, rows(k)]
        return remote(piece, piece, y_send.at[d, k], y_recv.at[d, k], req, at_y(sign[d]))

    def half_copy(k, d, arriving):
        owner = at_y(-2 * sign[d]) if arriving else at_y(-sign[d])
        piece = full.at[owner, pl.ds(d * SLOTS // 2, SLOTS // 2), rows(k)]
        return remote(piece, piece, half_send.at[d, k], half_recv.at[d, k], req, at_y(sign[d]))

    def sib_copy(k, part, arriving):
        core = 1 - c if arriving else c
        step = (0, -1, 1, 2)[part]
        piece = full.at[lax.rem(y + step + NY, NY) * 2 + core, :, rows(k)]
        return remote(piece, piece, sib_send.at[part, k], sib_recv.at[part, k], req, sibling)

    def source(step, j):
        request = order[at_x(step) * SLOTS + j]
        device = request // SLOTS
        return (device // NX) * SLOTS + request % SLOTS, device % NX

    table = {(s, j): source(s, j) for s in (-1, 0, 1, 2) for j in range(SLOTS)}

    def z_send_step(k, hop):
        for d in (0, 1):
            if hop == 1:
                if d == 0:
                    loads[k].wait()
            else:
                z_copy(k, hop - 1, d, True).wait_recv()
            z_copy(k, hop, d, False).start()

    def x_far(k):
        for d in (0, 1):
            z_copy(k, 4, d, True).wait_recv()
        for d in (0, 1):
            for i in range(SLOTS // 2):
                j = i + d * SLOTS // 2
                far_out[d, i, rows(k)] = held[k][table[2, j][0]]
            far_copy(k, d).start()

    def x_near(k):
        for d in (0, 1):
            far_copy(k, d).wait_recv()
            for j in range(SLOTS):
                index, column = table[sign[d], j]
                mine = held[k][index]
                i = j - d * SLOTS // 2
                if 0 <= i < SLOTS // 2:
                    mine = lax.select(column == x, mine, far_in[d, i, rows(k)])
                near_out[d, j, rows(k)] = mine
            near_copy(k, d).start()

    def x_done(k):
        for d in (0, 1):
            near_copy(k, d).wait_recv()
        for j in range(SLOTS):
            index, column = table[0, j]
            offset = lax.rem(column - x + NX, NX)
            if j < SLOTS // 2:
                from_left = offset >= 2
            else:
                from_left = offset == 3
            mine = held[k][index]
            other = lax.select(from_left, near_in[0, j, rows(k)], near_in[1, j, rows(k)])
            full[tp, j, rows(k)] = lax.select(offset == 0, mine, other)
        for d in (0, 1):
            y_copy(k, d, False).start()
        sib_copy(k, 0, False).start()

    def y_forward(k):
        for d in (0, 1):
            y_copy(k, d, True).wait_recv()
            half_copy(k, d, False).start()
            sib_copy(k, 1 + d, False).start()

    def y_finish(k):
        for d in (0, 1):
            half_copy(k, d, True).wait_recv()
        sib_copy(k, 3, False).start()

    events = []
    for k in range(CHUNKS):
        for hop in (1, 2, 3, 4):
            events.append((2 * k + hop, functools.partial(z_send_step, k, hop)))
        events.append((2 * k + 5.2, functools.partial(x_far, k)))
        events.append((2 * k + 6.1, functools.partial(x_near, k)))
        events.append((2 * k + 7.15, functools.partial(x_done, k)))
        events.append((2 * k + 8.2, functools.partial(y_forward, k)))
        events.append((2 * k + 9.1, functools.partial(y_finish, k)))
    for _, event in sorted(events, key=lambda item: item[0]):
        event()

    for k in range(CHUNKS):
        for part in range(4):
            sib_copy(k, part, True).wait_recv()
    for k in range(CHUNKS):
        for d in (0, 1):
            for hop in (1, 2, 3, 4):
                z_copy(k, hop, d, False).wait_send()
            far_copy(k, d).wait_send()
            near_copy(k, d).wait_send()
            y_copy(k, d, False).wait_send()
            half_copy(k, d, False).wait_send()
        for part in range(4):
            sib_copy(k, part, False).wait_send()


def deal(order, hidden):
    dma = pltpu.SemaphoreType.DMA
    packet = (ROWS, WIDTH)
    return pl.pallas_call(
        deal_kernel,
        out_shape=jax.ShapeDtypeStruct((TP, SLOTS, NODES, WIDTH), jnp.bfloat16),
        in_specs=[pl.BlockSpec(memory_space=pltpu.SMEM), pl.BlockSpec(memory_space=pl.ANY)],
        out_specs=pl.BlockSpec(memory_space=pltpu.VMEM),
        scratch_shapes=[pltpu.VMEM((NZ * SLOTS, *packet), jnp.bfloat16)] * CHUNKS + [
            pltpu.VMEM((2, SLOTS // 2, NODES, WIDTH), jnp.bfloat16),
            pltpu.VMEM((2, SLOTS // 2, NODES, WIDTH), jnp.bfloat16),
            pltpu.VMEM((2, SLOTS, NODES, WIDTH), jnp.bfloat16),
            pltpu.VMEM((2, SLOTS, NODES, WIDTH), jnp.bfloat16),
            dma((CHUNKS,)),
            dma((2, 4, CHUNKS)), dma((2, 4, CHUNKS)),
            dma((2, CHUNKS)), dma((2, CHUNKS)),
            dma((2, CHUNKS)), dma((2, CHUNKS)),
            dma((2, CHUNKS)), dma((2, CHUNKS)),
            dma((2, CHUNKS)), dma((2, CHUNKS)),
            dma((4, CHUNKS)), dma((4, CHUNKS)),
        ],
        compiler_params=pltpu.CompilerParams(
            collective_id=0, has_side_effects=True, vmem_limit_bytes=24 * 2**20
        ),
        name="deal",
    )(order, hidden)


def tree_kernel(lengths, parents, freq, ancestry, cosine, sine):
    low = lax.broadcasted_iota(jnp.int32, (NODES, NODES), 0)
    high = lax.broadcasted_iota(jnp.int32, (NODES, NODES), 1)
    eye = (low == high).astype(jnp.float32)
    lane = lax.broadcasted_iota(jnp.int32, (NODES, HEAD), 1)
    links = []
    for s in range(SLOTS):
        link = ((low == parents[s:s + 1, :]) & (high > 0)).astype(jnp.float32)
        links.append(jnp.minimum(eye + link, 1.0))
    for _ in range((NODES - 1).bit_length()):
        links = [
            jnp.minimum(
                jnp.dot(a.astype(jnp.bfloat16), a.astype(jnp.bfloat16), preferred_element_type=jnp.float32), 1.0
            )
            for a in links
        ]
    for s in range(SLOTS):
        above = links[s].T
        ancestry[s] = above
        depth = jnp.sum(above, axis=-1, keepdims=True)
        position = lengths[s].astype(jnp.float32) + depth - 1.0
        angle = position * freq[...]
        cosine[s] = jnp.cos(angle)
        turned = jnp.sin(angle)
        sine[s] = jnp.where(lane < HEAD // 2, -turned, turned)


def tree(lengths, parents):
    half = HEAD // 2
    freq = 500000.0 ** (-2.0 * np.arange(half, dtype=np.float64) / HEAD)
    freq = jnp.asarray(np.concatenate([freq, freq])[None].astype(np.float32))
    vmem = pl.BlockSpec(memory_space=pltpu.VMEM)
    return pl.pallas_call(
        tree_kernel,
        out_shape=(
            jax.ShapeDtypeStruct((SLOTS, NODES, NODES), jnp.float32),
            jax.ShapeDtypeStruct((SLOTS, NODES, HEAD), jnp.float32),
            jax.ShapeDtypeStruct((SLOTS, NODES, HEAD), jnp.float32),
        ),
        in_specs=[pl.BlockSpec(memory_space=pltpu.SMEM), vmem, vmem],
        out_specs=(vmem, vmem, vmem),
        name="tree",
    )(lengths, parents, freq)


def attend_kernel(lengths, kept, full, gain, ancestry, cosine, sine, w_query, w_key, w_value, key_cache, value_cache,
                  attended, appended, normed, wq, wk, wv, keys, values, q_rows, kv_rows, q_rot, fresh_k, fresh_v,
                  m_ref, l_ref, acc_ref, w_sem, kv_sem):
    loads = [
        pltpu.make_async_copy(src, dst, w_sem.at[i])
        for i, (src, dst) in enumerate(((w_query, wq), (w_key, wk), (w_value, wv)))
    ]
    for load in loads:
        load.start()

    def cache_loads(s):
        return (
            pltpu.make_async_copy(key_cache.at[s], keys.at[s], kv_sem.at[0, s]),
            pltpu.make_async_copy(value_cache.at[s], values.at[s], kv_sem.at[1, s]),
        )

    for s in range(SLOTS):
        for load in cache_loads(s):
            load.start()

    rows = SLOTS * NODES
    step = 128
    for r in range(0, rows, step):
        pieces = [full[t, r:r + step, :].astype(jnp.float32) for t in range(TP)]
        total = sum(jnp.sum(p * p, axis=-1, keepdims=True) for p in pieces)
        inverse = lax.rsqrt(total * (1.0 / (TP * WIDTH)) + EPS)
        for t in range(TP):
            scaled = pieces[t] * inverse * gain[:, t * WIDTH:(t + 1) * WIDTH].astype(jnp.float32)
            normed[r:r + step, t * WIDTH:(t + 1) * WIDTH] = scaled.astype(jnp.bfloat16)
    for load in loads:
        load.wait()
    q_rows[...] = jnp.dot(normed[...], wq[...], preferred_element_type=jnp.float32)
    kv_rows[:, :HEAD] = jnp.dot(normed[...], wk[...], preferred_element_type=jnp.float32)
    kv_rows[:, HEAD:] = jnp.dot(normed[...], wv[...], preferred_element_type=jnp.float32)

    kept_lane = lax.broadcasted_iota(jnp.int32, (KEEP, NODES), 1)
    kept_row = lax.broadcasted_iota(jnp.int32, (KEEP, NODES), 0)
    block_lane = lax.broadcasted_iota(jnp.int32, (1, BLOCK), 1)
    factor = SCALE * LOG2E

    @pl.loop(0, SLOTS)
    def _(s):
        node_rows = pl.ds(pl.multiple_of(s * NODES, NODES), NODES)
        co, si = cosine[s], sine[s]

        def rotated(u):
            return (u * co + pltpu.roll(u, HEAD // 2, 1) * si).astype(jnp.bfloat16)

        key = rotated(kv_rows[node_rows, :HEAD])
        value = kv_rows[node_rows, HEAD:].astype(jnp.bfloat16)
        select = kept_row * 0 + kept[s, 0]
        for k in range(1, KEEP):
            select = jnp.where(kept_row == k, kept[s, k], select)
        onehot = (select == kept_lane).astype(jnp.bfloat16)
        appended[s, 0] = jnp.dot(onehot, key, preferred_element_type=jnp.float32).astype(jnp.bfloat16)
        appended[s, 1] = jnp.dot(onehot, value, preferred_element_type=jnp.float32).astype(jnp.bfloat16)
        for h in range(3):
            q_rot[h * NODES:(h + 1) * NODES, :] = rotated(q_rows[node_rows, h * HEAD:(h + 1) * HEAD])
        query = q_rot[...]
        scores = lax.dot_general(query, key, (((1,), (1,)), ((), ())), preferred_element_type=jnp.float32)
        visible = jnp.concatenate([ancestry[s]] * 3, axis=0) > 0
        scores = jnp.where(visible, scores * factor, -jnp.inf)
        top = jnp.max(scores, axis=-1, keepdims=True)
        weight = jnp.exp2(scores - top)
        m_ref[...] = top
        l_ref[...] = jnp.sum(weight, axis=-1, keepdims=True)
        acc_ref[...] = jnp.dot(weight.astype(jnp.bfloat16), value, preferred_element_type=jnp.float32)
        for load in cache_loads(s):
            load.wait()
        length = lengths[s]

        def block(b, masked):
            span = pl.ds(pl.multiple_of(b * BLOCK, BLOCK), BLOCK)
            sc = lax.dot_general(
                query, keys[s, span, :], (((1,), (1,)), ((), ())), preferred_element_type=jnp.float32
            ) * factor
            if masked:
                sc = jnp.where(block_lane < length - b * BLOCK, sc, -jnp.inf)
            old = m_ref[...]
            new = jnp.maximum(old, jnp.max(sc, axis=-1, keepdims=True))
            shrink = jnp.exp2(old - new)
            p = jnp.exp2(sc - new)
            m_ref[...] = new
            l_ref[...] = l_ref[...] * shrink + jnp.sum(p, axis=-1, keepdims=True)
            acc_ref[...] = acc_ref[...] * shrink + jnp.dot(
                p.astype(jnp.bfloat16), values[s, span, :], preferred_element_type=jnp.float32
            )

        whole = length // BLOCK

        @pl.loop(0, whole)
        def _(b):
            block(b, False)

        @pl.when(whole * BLOCK < length)
        def _():
            block(whole, True)

        result = (acc_ref[...] / l_ref[...]).astype(jnp.bfloat16)
        for h in range(3):
            attended[node_rows, h * HEAD:(h + 1) * HEAD] = result[h * NODES:(h + 1) * NODES]


def attend(lengths, kept, full, gain, tables, w_query, w_key, w_value, key_cache, value_cache):
    vmem = pl.BlockSpec(memory_space=pltpu.VMEM)
    smem = pl.BlockSpec(memory_space=pltpu.SMEM)
    hbm = pl.BlockSpec(memory_space=pl.ANY)
    rows = SLOTS * NODES
    bf16, f32 = jnp.bfloat16, jnp.float32
    model = TP * WIDTH
    return pl.pallas_call(
        attend_kernel,
        out_shape=(
            jax.ShapeDtypeStruct((rows, WIDTH), bf16),
            jax.ShapeDtypeStruct((SLOTS, 2, KEEP, HEAD), bf16),
        ),
        in_specs=[smem, smem, vmem, vmem, vmem, vmem, vmem] + [hbm] * 5,
        out_specs=(vmem, vmem),
        scratch_shapes=[
            pltpu.VMEM((rows, model), bf16),
            pltpu.VMEM((model, WIDTH), bf16),
            pltpu.VMEM((model, HEAD), bf16),
            pltpu.VMEM((model, HEAD), bf16),
            pltpu.VMEM((SLOTS, CACHE, HEAD), bf16),
            pltpu.VMEM((SLOTS, CACHE, HEAD), bf16),
            pltpu.VMEM((rows, WIDTH), f32),
            pltpu.VMEM((rows, 2 * HEAD), f32),
            pltpu.VMEM((3 * NODES, HEAD), bf16),
            pltpu.VMEM((NODES, HEAD), bf16),
            pltpu.VMEM((NODES, HEAD), bf16),
            pltpu.VMEM((3 * NODES, 1), f32),
            pltpu.VMEM((3 * NODES, 1), f32),
            pltpu.VMEM((3 * NODES, HEAD), f32),
            pltpu.SemaphoreType.DMA((3,)),
            pltpu.SemaphoreType.DMA((2, SLOTS)),
        ],
        compiler_params=pltpu.CompilerParams(vmem_limit_bytes=48 * 2**20),
        name="attend",
    )(lengths, kept, full, gain, *tables, w_query, w_key, w_value, key_cache, value_cache)


PARTS = 3
PROWS = SLOTS * NODES // PARTS
PHALF = PROWS // 2


def project_kernel(attended, w_out, dealt, out, sib_out, sib_in, own, far_out, far_in, near_out, near_in,
                   sib_send, sib_recv, far_send, far_recv, near_send, near_recv):
    req, tp, z, x, y, c = place()
    sign = (1, -1)
    sibling = y * 2 + 1 - c

    def at_y(step):
        return lax.rem(y + step + NY, NY) * 2 + c

    greet([(req, at_y(1)), (req, at_y(-1)), (req, sibling)])

    def term(r, step, core):
        target = lax.rem(y + step + NY, NY) * 2 + core
        columns = pl.ds(pl.multiple_of(target * WIDTH, 128), WIDTH)
        return jnp.dot(
            attended[r * PROWS:(r + 1) * PROWS, :], w_out[:, columns], preferred_element_type=jnp.float32
        )

    def sib_copy(r, i):
        return remote(sib_out.at[r, i], sib_in.at[r, i], sib_send.at[r, i], sib_recv.at[r, i], req, sibling)

    def far_copy(r, d):
        return remote(far_out.at[r, d], far_in.at[r, d], far_send.at[r, d], far_recv.at[r, d], req, at_y(sign[d]))

    def near_copy(r, d):
        return remote(near_out.at[r, d], near_in.at[r, d], near_send.at[r, d], near_recv.at[r, d], req, at_y(sign[d]))

    steps = (2, 1, -1, 0)

    def first(r):
        for i, step in enumerate(steps):
            sib_out[r, i] = term(r, step, 1 - c).astype(jnp.bfloat16)
            sib_copy(r, i).start()
        for i, step in enumerate(steps):
            own[r, i] = term(r, step, c)

    def pair(r, i):
        sib_copy(r, i).wait_recv()
        return own[r, i] + sib_in[r, i].astype(jnp.float32)

    def far(r):
        both = pair(r, 0).astype(jnp.bfloat16)
        for d in (0, 1):
            far_out[r, d] = both[d * PHALF:(d + 1) * PHALF]
            far_copy(r, d).start()

    def near(r):
        for d in (0, 1):
            mine = pair(r, 1 + d)
            far_copy(r, d).wait_recv()
            lo, hi = d * PHALF, (d + 1) * PHALF
            rest = slice(PHALF, PROWS) if d == 0 else slice(0, PHALF)
            near_out[r, d, lo:hi] = (mine[lo:hi] + far_in[r, d].astype(jnp.float32)).astype(jnp.bfloat16)
            near_out[r, d, rest] = mine[rest].astype(jnp.bfloat16)
            near_copy(r, d).start()

    def last(r):
        mine = pair(r, 3) + dealt[r * PROWS:(r + 1) * PROWS, :].astype(jnp.float32)
        for d in (0, 1):
            near_copy(r, d).wait_recv()
            mine = mine + near_in[r, d].astype(jnp.float32)
        out[r * PROWS:(r + 1) * PROWS, :] = mine.astype(jnp.bfloat16)

    first(0)
    far(0)
    first(1)
    far(1)
    near(0)
    first(2)
    far(2)
    near(1)
    last(0)
    near(2)
    last(1)
    last(2)
    for r in range(PARTS):
        for i in range(4):
            sib_copy(r, i).wait_send()
        for d in (0, 1):
            far_copy(r, d).wait_send()
            near_copy(r, d).wait_send()


def project(attended, w_out, dealt):
    vmem = pl.BlockSpec(memory_space=pltpu.VMEM)
    bf16 = jnp.bfloat16
    dma = pltpu.SemaphoreType.DMA
    return pl.pallas_call(
        project_kernel,
        out_shape=jax.ShapeDtypeStruct((SLOTS * NODES, WIDTH), bf16),
        in_specs=[vmem] * 3,
        out_specs=vmem,
        scratch_shapes=[
            pltpu.VMEM((PARTS, 4, PROWS, WIDTH), bf16),
            pltpu.VMEM((PARTS, 4, PROWS, WIDTH), bf16),
            pltpu.VMEM((PARTS, 4, PROWS, WIDTH), jnp.float32),
            pltpu.VMEM((PARTS, 2, PHALF, WIDTH), bf16),
            pltpu.VMEM((PARTS, 2, PHALF, WIDTH), bf16),
            pltpu.VMEM((PARTS, 2, PROWS, WIDTH), bf16),
            pltpu.VMEM((PARTS, 2, PROWS, WIDTH), bf16),
            dma((PARTS, 4)), dma((PARTS, 4)),
            dma((PARTS, 2)), dma((PARTS, 2)),
            dma((PARTS, 2)), dma((PARTS, 2)),
        ],
        compiler_params=pltpu.CompilerParams(
            collective_id=1, has_side_effects=True, vmem_limit_bytes=24 * 2**20
        ),
        name="project",
    )(attended, w_out, dealt)


def body(hidden_in, request_order, norm_gain, w_query, key_weight, value_weight, w_out,
         key_cache, cached_values, cache_lengths, tree_parent, kept_nodes):
    rows = SLOTS * NODES
    tables = tree(cache_lengths, tree_parent)
    full = deal(request_order, hidden_in).reshape(TP, rows, WIDTH)
    attended, appended = attend(
        cache_lengths, kept_nodes, full, norm_gain.reshape(1, -1), tables, w_query, key_weight, value_weight,
        key_cache.reshape(SLOTS, CACHE, HEAD), cached_values.reshape(SLOTS, CACHE, HEAD),
    )
    dealt = lax.dynamic_index_in_dim(full, lax.axis_index("tp"), 0, keepdims=False)
    layer_out = project(attended, w_out, dealt)
    return layer_out.reshape(SLOTS, NODES, WIDTH), appended.reshape(SLOTS, 2, KEEP, 1, HEAD)


def solution(mesh):
    placed = (
        P("req", None, "tp"), P(), P(), P(None, "tp"), P(None, "tp"), P(None, "tp"), P("tp", None),
        P("req", "tp", None, None), P("req", "tp", None, None), P("req"), P("req", None), P("req", None),
    )
    return jax.shard_map(
        body,
        mesh=mesh,
        in_specs=placed,
        out_specs=(P("req", None, "tp"), P("req", None, None, "tp", None)),
        check_vma=False,
    )
```

```python
import functools
import math

import jax
import jax.numpy as jnp
import numpy as np
from jax import lax
from jax.experimental import pallas as pl
from jax.experimental.pallas import tpu as pltpu
from jax.sharding import PartitionSpec as P

MESH = pl.DeviceIdType.MESH
HEAD = 128
EPS = 1e-05
SLOTS, NODES, WIDTH = 6, 64, 384
NX, NZ, NY = 4, 8, 4
TP = 8
CACHE = 3456
KEEP = 8
CHUNKS = 4
ROWS = NODES // CHUNKS
BLOCK = 384
SHORTEST = 3
LOG2E = math.log2(math.e)
SCALE = HEAD ** (-0.5)


def remote(src, dst, send, recv, req, tp):
    return pltpu.make_async_remote_copy(
        src_ref=src, dst_ref=dst, send_sem=send, recv_sem=recv,
        device_id=(req, tp), device_id_type=MESH,
    )


def place():
    req = lax.axis_index("req")
    tp = lax.axis_index("tp")
    return req, tp, req // NX, req % NX, tp // 2, tp % 2


def greet(peers):
    barrier = pltpu.get_barrier_semaphore()
    for req, tp in peers:
        pl.semaphore_signal(barrier, inc=1, device_id=(req, tp), device_id_type=MESH)
    pl.semaphore_wait(barrier, len(peers))


def deal_kernel(order, hidden, full, *scratch):
    held = scratch[:CHUNKS]
    far_out, far_in, near_out, near_in = scratch[CHUNKS:CHUNKS + 4]
    (load_sem, z_send, z_recv, far_send, far_recv, near_send, near_recv,
     y_send, y_recv, half_send, half_recv, sib_send, sib_recv) = scratch[CHUNKS + 4:]
    req, tp, z, x, y, c = place()

    def at_z(step):
        return lax.rem(z + step + NZ, NZ) * NX + x

    def at_x(step):
        return z * NX + lax.rem(x + step + NX, NX)

    def at_y(step):
        return lax.rem(y + step + NY, NY) * 2 + c

    sign = (1, -1)
    sibling = y * 2 + 1 - c

    loads = [
        pltpu.make_async_copy(
            hidden.at[:, pl.ds(k * ROWS, ROWS), :], held[k].at[pl.ds(z * SLOTS, SLOTS)], load_sem.at[k]
        )
        for k in range(CHUNKS)
    ]
    for load in loads:
        load.start()
    greet([(at_z(1), tp), (at_z(-1), tp), (at_x(1), tp), (at_x(-1), tp),
           (req, at_y(1)), (req, at_y(-1)), (req, sibling)])

    def z_copy(k, hop, d, arriving):
        back = hop if arriving else hop - 1
        owner = lax.rem(z - sign[d] * back + 2 * NZ, NZ)
        count = SLOTS if hop < 4 else SLOTS // 2
        first = 0 if hop < 4 or d == 0 else SLOTS // 2
        block = held[k].at[pl.ds(owner * SLOTS + first, count)]
        return remote(block, block, z_send.at[d, hop - 1, k], z_recv.at[d, hop - 1, k], at_z(sign[d]), tp)

    def rows(k):
        return pl.ds(k * ROWS, ROWS)

    def far_copy(k, d):
        return remote(far_out.at[d, :, rows(k)], far_in.at[d, :, rows(k)],
                      far_send.at[d, k], far_recv.at[d, k], at_x(sign[d]), tp)

    def near_copy(k, d):
        return remote(near_out.at[d, :, rows(k)], near_in.at[d, :, rows(k)],
                      near_send.at[d, k], near_recv.at[d, k], at_x(sign[d]), tp)

    def y_copy(k, d, arriving):
        piece = full.at[at_y(-sign[d]) if arriving else tp, :, rows(k)]
        return remote(piece, piece, y_send.at[d, k], y_recv.at[d, k], req, at_y(sign[d]))

    def half_copy(k, d, arriving):
        owner = at_y(-2 * sign[d]) if arriving else at_y(-sign[d])
        piece = full.at[owner, pl.ds(d * SLOTS // 2, SLOTS // 2), rows(k)]
        return remote(piece, piece, half_send.at[d, k], half_recv.at[d, k], req, at_y(sign[d]))

    def sib_copy(k, part, arriving):
        core = 1 - c if arriving else c
        step = (0, -1, 1, 2)[part]
        piece = full.at[lax.rem(y + step + NY, NY) * 2 + core, :, rows(k)]
        return remote(piece, piece, sib_send.at[part, k], sib_recv.at[part, k], req, sibling)

    def source(step, j):
        request = order[at_x(step) * SLOTS + j]
        device = request // SLOTS
        return (device // NX) * SLOTS + request % SLOTS, device % NX

    table = {(s, j): source(s, j) for s in (-1, 0, 1, 2) for j in range(SLOTS)}

    def z_send_step(k, hop):
        for d in (0, 1):
            if hop == 1:
                if d == 0:
                    loads[k].wait()
            else:
                z_copy(k, hop - 1, d, True).wait_recv()
            z_copy(k, hop, d, False).start()

    def x_far(k):
        for d in (0, 1):
            z_copy(k, 4, d, True).wait_recv()
        for d in (0, 1):
            for i in range(SLOTS // 2):
                j = i + d * SLOTS // 2
                far_out[d, i, rows(k)] = held[k][table[2, j][0]]
            far_copy(k, d).start()

    def x_near(k):
        for d in (0, 1):
            far_copy(k, d).wait_recv()
            for j in range(SLOTS):
                index, column = table[sign[d], j]
                mine = held[k][index]
                i = j - d * SLOTS // 2
                if 0 <= i < SLOTS // 2:
                    mine = lax.select(column == x, mine, far_in[d, i, rows(k)])
                near_out[d, j, rows(k)] = mine
            near_copy(k, d).start()

    def x_done(k):
        for d in (0, 1):
            near_copy(k, d).wait_recv()
        for j in range(SLOTS):
            index, column = table[0, j]
            offset = lax.rem(column - x + NX, NX)
            if j < SLOTS // 2:
                from_left = offset >= 2
            else:
                from_left = offset == 3
            mine = held[k][index]
            other = lax.select(from_left, near_in[0, j, rows(k)], near_in[1, j, rows(k)])
            full[tp, j, rows(k)] = lax.select(offset == 0, mine, other)
        for d in (0, 1):
            y_copy(k, d, False).start()
        sib_copy(k, 0, False).start()

    def y_forward(k):
        for d in (0, 1):
            y_copy(k, d, True).wait_recv()
            half_copy(k, d, False).start()
            sib_copy(k, 1 + d, False).start()

    def y_finish(k):
        for d in (0, 1):
            half_copy(k, d, True).wait_recv()
        sib_copy(k, 3, False).start()

    events = []
    for k in range(CHUNKS):
        for hop in (1, 2, 3, 4):
            events.append((2 * k + hop, functools.partial(z_send_step, k, hop)))
        events.append((2 * k + 5.2, functools.partial(x_far, k)))
        events.append((2 * k + 6.1, functools.partial(x_near, k)))
        events.append((2 * k + 7.15, functools.partial(x_done, k)))
        events.append((2 * k + 8.2, functools.partial(y_forward, k)))
        events.append((2 * k + 9.1, functools.partial(y_finish, k)))
    for _, event in sorted(events, key=lambda item: item[0]):
        event()

    for k in range(CHUNKS):
        for part in range(4):
            sib_copy(k, part, True).wait_recv()
    for k in range(CHUNKS):
        for d in (0, 1):
            for hop in (1, 2, 3, 4):
                z_copy(k, hop, d, False).wait_send()
            far_copy(k, d).wait_send()
            near_copy(k, d).wait_send()
            y_copy(k, d, False).wait_send()
            half_copy(k, d, False).wait_send()
        for part in range(4):
            sib_copy(k, part, False).wait_send()


def deal(order, hidden):
    dma = pltpu.SemaphoreType.DMA
    packet = (ROWS, WIDTH)
    return pl.pallas_call(
        deal_kernel,
        out_shape=jax.ShapeDtypeStruct((TP, SLOTS, NODES, WIDTH), jnp.bfloat16),
        in_specs=[pl.BlockSpec(memory_space=pltpu.SMEM), pl.BlockSpec(memory_space=pl.ANY)],
        out_specs=pl.BlockSpec(memory_space=pltpu.VMEM),
        scratch_shapes=[pltpu.VMEM((NZ * SLOTS, *packet), jnp.bfloat16)] * CHUNKS + [
            pltpu.VMEM((2, SLOTS // 2, NODES, WIDTH), jnp.bfloat16),
            pltpu.VMEM((2, SLOTS // 2, NODES, WIDTH), jnp.bfloat16),
            pltpu.VMEM((2, SLOTS, NODES, WIDTH), jnp.bfloat16),
            pltpu.VMEM((2, SLOTS, NODES, WIDTH), jnp.bfloat16),
            dma((CHUNKS,)),
            dma((2, 4, CHUNKS)), dma((2, 4, CHUNKS)),
            dma((2, CHUNKS)), dma((2, CHUNKS)),
            dma((2, CHUNKS)), dma((2, CHUNKS)),
            dma((2, CHUNKS)), dma((2, CHUNKS)),
            dma((2, CHUNKS)), dma((2, CHUNKS)),
            dma((4, CHUNKS)), dma((4, CHUNKS)),
        ],
        compiler_params=pltpu.CompilerParams(
            collective_id=0, has_side_effects=True, vmem_limit_bytes=24 * 2**20
        ),
        name="deal",
    )(order, hidden)


def tree_kernel(lengths, parents, freq, ancestry, cosine, sine):
    low = lax.broadcasted_iota(jnp.int32, (NODES, NODES), 0)
    high = lax.broadcasted_iota(jnp.int32, (NODES, NODES), 1)
    eye = (low == high).astype(jnp.float32)
    lane = lax.broadcasted_iota(jnp.int32, (NODES, HEAD), 1)
    links = []
    for s in range(SLOTS):
        link = ((low == parents[s:s + 1, :]) & (high > 0)).astype(jnp.float32)
        links.append(jnp.minimum(eye + link, 1.0))
    for _ in range((NODES - 1).bit_length()):
        links = [
            jnp.minimum(
                jnp.dot(a.astype(jnp.bfloat16), a.astype(jnp.bfloat16), preferred_element_type=jnp.float32), 1.0
            )
            for a in links
        ]
    for s in range(SLOTS):
        above = links[s].T
        ancestry[s] = above
        depth = jnp.sum(above, axis=-1, keepdims=True)
        position = lengths[s].astype(jnp.float32) + depth - 1.0
        angle = position * freq[...]
        cosine[s] = jnp.cos(angle)
        turned = jnp.sin(angle)
        sine[s] = jnp.where(lane < HEAD // 2, -turned, turned)


def tree(lengths, parents):
    half = HEAD // 2
    freq = 500000.0 ** (-2.0 * np.arange(half, dtype=np.float64) / HEAD)
    freq = jnp.asarray(np.concatenate([freq, freq])[None].astype(np.float32))
    vmem = pl.BlockSpec(memory_space=pltpu.VMEM)
    return pl.pallas_call(
        tree_kernel,
        out_shape=(
            jax.ShapeDtypeStruct((SLOTS, NODES, NODES), jnp.float32),
            jax.ShapeDtypeStruct((SLOTS, NODES, HEAD), jnp.float32),
            jax.ShapeDtypeStruct((SLOTS, NODES, HEAD), jnp.float32),
        ),
        in_specs=[pl.BlockSpec(memory_space=pltpu.SMEM), vmem, vmem],
        out_specs=(vmem, vmem, vmem),
        name="tree",
    )(lengths, parents, freq)


def attend_kernel(lengths, kept, full, gain, ancestry, cosine, sine, w_query, w_key, w_value, key_cache, value_cache,
                  attended, appended, normed, wq, wk, wv, keys, values, q_rows, kv_rows, q_rot, fresh_k, fresh_v,
                  raw, w_sem, kv_sem):
    loads = [
        pltpu.make_async_copy(src, dst, w_sem.at[i])
        for i, (src, dst) in enumerate(((w_query, wq), (w_key, wk), (w_value, wv)))
    ]
    for load in loads:
        load.start()

    def cache_loads(s):
        return (
            pltpu.make_async_copy(key_cache.at[s], keys.at[s], kv_sem.at[0, s]),
            pltpu.make_async_copy(value_cache.at[s], values.at[s], kv_sem.at[1, s]),
        )

    for s in range(SLOTS):
        for load in cache_loads(s):
            load.start()

    rows = SLOTS * NODES
    step = 128
    for r in range(0, rows, step):
        pieces = [full[t, r:r + step, :].astype(jnp.float32) for t in range(TP)]
        total = sum(jnp.sum(p * p, axis=-1, keepdims=True) for p in pieces)
        inverse = lax.rsqrt(total * (1.0 / (TP * WIDTH)) + EPS)
        for t in range(TP):
            scaled = pieces[t] * inverse * gain[:, t * WIDTH:(t + 1) * WIDTH].astype(jnp.float32)
            normed[r:r + step, t * WIDTH:(t + 1) * WIDTH] = scaled.astype(jnp.bfloat16)
    for load in loads:
        load.wait()
    q_rows[...] = jnp.dot(normed[...], wq[...], preferred_element_type=jnp.float32)
    kv_rows[:, :HEAD] = jnp.dot(normed[...], wk[...], preferred_element_type=jnp.float32)
    kv_rows[:, HEAD:] = jnp.dot(normed[...], wv[...], preferred_element_type=jnp.float32)

    kept_lane = lax.broadcasted_iota(jnp.int32, (KEEP, NODES), 1)
    kept_row = lax.broadcasted_iota(jnp.int32, (KEEP, NODES), 0)
    block_lane = lax.broadcasted_iota(jnp.int32, (1, BLOCK), 1)
    factor = SCALE * LOG2E
    transposed = (((1,), (1,)), ((), ()))

    for s in range(SLOTS):
        node_rows = slice(s * NODES, (s + 1) * NODES)
        co, si = cosine[s], sine[s]

        def rotated(u):
            return (u * co + pltpu.roll(u, HEAD // 2, 1) * si).astype(jnp.bfloat16)

        key = rotated(kv_rows[node_rows, :HEAD])
        value = kv_rows[node_rows, HEAD:].astype(jnp.bfloat16)
        fresh_k[s] = key
        fresh_v[s] = value
        select = kept_row * 0 + kept[s, 0]
        for k in range(1, KEEP):
            select = jnp.where(kept_row == k, kept[s, k], select)
        onehot = (select == kept_lane).astype(jnp.bfloat16)
        appended[s, 0] = jnp.dot(onehot, key, preferred_element_type=jnp.float32).astype(jnp.bfloat16)
        appended[s, 1] = jnp.dot(onehot, value, preferred_element_type=jnp.float32).astype(jnp.bfloat16)
        for h in range(3):
            q_rot[s, h * NODES:(h + 1) * NODES, :] = rotated(q_rows[node_rows, h * HEAD:(h + 1) * HEAD])

    def slot(s, length, count):
        query = q_rot[s]
        visible = ancestry[s] > 0
        tree_scores = lax.dot_general(query, fresh_k[s], transposed, preferred_element_type=jnp.float32)
        tree_scores = jnp.concatenate(
            [
                jnp.where(visible, tree_scores[h * NODES:(h + 1) * NODES], -jnp.inf)
                for h in range(3)
            ],
            axis=0,
        )
        best = None
        for b in range(count):
            sc = lax.dot_general(
                query, keys[s, b * BLOCK:(b + 1) * BLOCK, :], transposed, preferred_element_type=jnp.float32
            )
            if b == count - 1 or count == SHORTEST:
                sc = jnp.where(block_lane < length - b * BLOCK, sc, -jnp.inf)
            raw[b] = sc
            for i in range(BLOCK // HEAD):
                part = sc[:, i * HEAD:(i + 1) * HEAD]
                best = part if best is None else jnp.maximum(best, part)
        top = jnp.maximum(
            jnp.max(tree_scores, axis=-1, keepdims=True), jnp.max(best, axis=-1, keepdims=True)
        ) * factor
        weight = jnp.exp2(tree_scores * factor - top)
        small = jnp.sum(weight, axis=-1, keepdims=True)
        acc = jnp.dot(weight.astype(jnp.bfloat16), fresh_v[s], preferred_element_type=jnp.float32)
        total = None
        for b in range(count):
            p = jnp.exp2(raw[b] * factor - top)
            for i in range(BLOCK // HEAD):
                part = p[:, i * HEAD:(i + 1) * HEAD]
                total = part if total is None else total + part
            acc = acc + jnp.dot(
                p.astype(jnp.bfloat16), values[s, b * BLOCK:(b + 1) * BLOCK, :], preferred_element_type=jnp.float32
            )
        small = small + jnp.sum(total, axis=-1, keepdims=True)
        result = (acc / small).astype(jnp.bfloat16)
        node_rows = pl.ds(pl.multiple_of(s * NODES, NODES), NODES)
        for h in range(3):
            attended[node_rows, h * HEAD:(h + 1) * HEAD] = result[h * NODES:(h + 1) * NODES]

    @pl.loop(0, SLOTS)
    def _(s):
        for load in cache_loads(s):
            load.wait()
        length = lengths[s]
        blocks = jnp.maximum((length + BLOCK - 1) // BLOCK, SHORTEST)
        for count in range(SHORTEST, CACHE // BLOCK + 1):
            @pl.when(blocks == count)
            def _():
                slot(s, length, count)


def attend(lengths, kept, full, gain, tables, w_query, w_key, w_value, key_cache, value_cache):
    vmem = pl.BlockSpec(memory_space=pltpu.VMEM)
    smem = pl.BlockSpec(memory_space=pltpu.SMEM)
    hbm = pl.BlockSpec(memory_space=pl.ANY)
    rows = SLOTS * NODES
    bf16, f32 = jnp.bfloat16, jnp.float32
    model = TP * WIDTH
    return pl.pallas_call(
        attend_kernel,
        out_shape=(
            jax.ShapeDtypeStruct((rows, WIDTH), bf16),
            jax.ShapeDtypeStruct((SLOTS, 2, KEEP, HEAD), bf16),
        ),
        in_specs=[smem, smem, vmem, vmem, vmem, vmem, vmem] + [hbm] * 5,
        out_specs=(vmem, vmem),
        scratch_shapes=[
            pltpu.VMEM((rows, model), bf16),
            pltpu.VMEM((model, WIDTH), bf16),
            pltpu.VMEM((model, HEAD), bf16),
            pltpu.VMEM((model, HEAD), bf16),
            pltpu.VMEM((SLOTS, CACHE, HEAD), bf16),
            pltpu.VMEM((SLOTS, CACHE, HEAD), bf16),
            pltpu.VMEM((rows, WIDTH), f32),
            pltpu.VMEM((rows, 2 * HEAD), f32),
            pltpu.VMEM((SLOTS, 3 * NODES, HEAD), bf16),
            pltpu.VMEM((SLOTS, NODES, HEAD), bf16),
            pltpu.VMEM((SLOTS, NODES, HEAD), bf16),
            pltpu.VMEM((CACHE // BLOCK, 3 * NODES, BLOCK), f32),
            pltpu.SemaphoreType.DMA((3,)),
            pltpu.SemaphoreType.DMA((2, SLOTS)),
        ],
        compiler_params=pltpu.CompilerParams(vmem_limit_bytes=48 * 2**20),
        name="attend",
    )(lengths, kept, full, gain, *tables, w_query, w_key, w_value, key_cache, value_cache)


PARTS = 3
PROWS = SLOTS * NODES // PARTS
PHALF = PROWS // 2


def project_kernel(attended, w_out, dealt, out, sib_out, sib_in, own, far_out, far_in, near_out, near_in,
                   sib_send, sib_recv, far_send, far_recv, near_send, near_recv):
    req, tp, z, x, y, c = place()
    sign = (1, -1)
    sibling = y * 2 + 1 - c

    def at_y(step):
        return lax.rem(y + step + NY, NY) * 2 + c

    greet([(req, at_y(1)), (req, at_y(-1)), (req, sibling)])

    def term(r, step, core):
        target = lax.rem(y + step + NY, NY) * 2 + core
        columns = pl.ds(pl.multiple_of(target * WIDTH, 128), WIDTH)
        return jnp.dot(
            attended[r * PROWS:(r + 1) * PROWS, :], w_out[:, columns], preferred_element_type=jnp.float32
        )

    def sib_copy(r, i):
        return remote(sib_out.at[r, i], sib_in.at[r, i], sib_send.at[r, i], sib_recv.at[r, i], req, sibling)

    def far_copy(r, d):
        return remote(far_out.at[r, d], far_in.at[r, d], far_send.at[r, d], far_recv.at[r, d], req, at_y(sign[d]))

    def near_copy(r, d):
        return remote(near_out.at[r, d], near_in.at[r, d], near_send.at[r, d], near_recv.at[r, d], req, at_y(sign[d]))

    steps = (2, 1, -1, 0)

    def first(r):
        for i, step in enumerate(steps):
            sib_out[r, i] = term(r, step, 1 - c).astype(jnp.bfloat16)
            sib_copy(r, i).start()
        for i, step in enumerate(steps):
            own[r, i] = term(r, step, c)

    def pair(r, i):
        sib_copy(r, i).wait_recv()
        return own[r, i] + sib_in[r, i].astype(jnp.float32)

    def far(r):
        both = pair(r, 0).astype(jnp.bfloat16)
        for d in (0, 1):
            far_out[r, d] = both[d * PHALF:(d + 1) * PHALF]
            far_copy(r, d).start()

    def near(r):
        for d in (0, 1):
            mine = pair(r, 1 + d)
            far_copy(r, d).wait_recv()
            lo, hi = d * PHALF, (d + 1) * PHALF
            rest = slice(PHALF, PROWS) if d == 0 else slice(0, PHALF)
            near_out[r, d, lo:hi] = (mine[lo:hi] + far_in[r, d].astype(jnp.float32)).astype(jnp.bfloat16)
            near_out[r, d, rest] = mine[rest].astype(jnp.bfloat16)
            near_copy(r, d).start()

    def last(r):
        mine = pair(r, 3) + dealt[r * PROWS:(r + 1) * PROWS, :].astype(jnp.float32)
        for d in (0, 1):
            near_copy(r, d).wait_recv()
            mine = mine + near_in[r, d].astype(jnp.float32)
        out[r * PROWS:(r + 1) * PROWS, :] = mine.astype(jnp.bfloat16)

    first(0)
    far(0)
    first(1)
    far(1)
    near(0)
    first(2)
    far(2)
    near(1)
    last(0)
    near(2)
    last(1)
    last(2)
    for r in range(PARTS):
        for i in range(4):
            sib_copy(r, i).wait_send()
        for d in (0, 1):
            far_copy(r, d).wait_send()
            near_copy(r, d).wait_send()


def project(attended, w_out, dealt):
    vmem = pl.BlockSpec(memory_space=pltpu.VMEM)
    bf16 = jnp.bfloat16
    dma = pltpu.SemaphoreType.DMA
    return pl.pallas_call(
        project_kernel,
        out_shape=jax.ShapeDtypeStruct((SLOTS * NODES, WIDTH), bf16),
        in_specs=[vmem] * 3,
        out_specs=vmem,
        scratch_shapes=[
            pltpu.VMEM((PARTS, 4, PROWS, WIDTH), bf16),
            pltpu.VMEM((PARTS, 4, PROWS, WIDTH), bf16),
            pltpu.VMEM((PARTS, 4, PROWS, WIDTH), jnp.float32),
            pltpu.VMEM((PARTS, 2, PHALF, WIDTH), bf16),
            pltpu.VMEM((PARTS, 2, PHALF, WIDTH), bf16),
            pltpu.VMEM((PARTS, 2, PROWS, WIDTH), bf16),
            pltpu.VMEM((PARTS, 2, PROWS, WIDTH), bf16),
            dma((PARTS, 4)), dma((PARTS, 4)),
            dma((PARTS, 2)), dma((PARTS, 2)),
            dma((PARTS, 2)), dma((PARTS, 2)),
        ],
        compiler_params=pltpu.CompilerParams(
            collective_id=1, has_side_effects=True, vmem_limit_bytes=24 * 2**20
        ),
        name="project",
    )(attended, w_out, dealt)


def body(hidden_in, request_order, norm_gain, w_query, key_weight, value_weight, w_out,
         key_cache, cached_values, cache_lengths, tree_parent, kept_nodes):
    rows = SLOTS * NODES
    tables = tree(cache_lengths, tree_parent)
    full = deal(request_order, hidden_in).reshape(TP, rows, WIDTH)
    attended, appended = attend(
        cache_lengths, kept_nodes, full, norm_gain.reshape(1, -1), tables, w_query, key_weight, value_weight,
        key_cache.reshape(SLOTS, CACHE, HEAD), cached_values.reshape(SLOTS, CACHE, HEAD),
    )
    dealt = lax.dynamic_index_in_dim(full, lax.axis_index("tp"), 0, keepdims=False)
    layer_out = project(attended, w_out, dealt)
    return layer_out.reshape(SLOTS, NODES, WIDTH), appended.reshape(SLOTS, 2, KEEP, 1, HEAD)


def solution(mesh):
    placed = (
        P("req", None, "tp"), P(), P(), P(None, "tp"), P(None, "tp"), P(None, "tp"), P("tp", None),
        P("req", "tp", None, None), P("req", "tp", None, None), P("req"), P("req", None), P("req", None),
    )
    return jax.shard_map(
        body,
        mesh=mesh,
        in_specs=placed,
        out_specs=(P("req", None, "tp"), P("req", None, None, "tp", None)),
        check_vma=False,
    )
```

```python
import functools
import math

import jax
import jax.numpy as jnp
import numpy as np
from jax import lax
from jax.experimental import pallas as pl
from jax.experimental.pallas import tpu as pltpu
from jax.sharding import PartitionSpec as P

MESH = pl.DeviceIdType.MESH
HEAD = 128
EPS = 1e-05
SLOTS, NODES, WIDTH = 6, 64, 384
NX, NZ, NY = 4, 8, 4
TP = 8
CACHE = 3456
KEEP = 8
SIZES = (32, 24, 8)
STARTS = (0, 32, 56)
CHUNKS = len(SIZES)
ORDER = (1, 11, 2, 12, 3, 13, 4, 21, 14, 5, 22, 15, 23, 6, 16, 24, 7, 25, 17, 26, 27, 8, 18, 28, 9, 19, 29)
BLOCK = 384
SHORTEST = 3
LOG2E = math.log2(math.e)
SCALE = HEAD ** (-0.5)


def remote(src, dst, send, recv, req, tp):
    return pltpu.make_async_remote_copy(
        src_ref=src, dst_ref=dst, send_sem=send, recv_sem=recv,
        device_id=(req, tp), device_id_type=MESH,
    )


def place():
    req = lax.axis_index("req")
    tp = lax.axis_index("tp")
    return req, tp, req // NX, req % NX, tp // 2, tp % 2


def greet(peers):
    barrier = pltpu.get_barrier_semaphore()
    for req, tp in peers:
        pl.semaphore_signal(barrier, inc=1, device_id=(req, tp), device_id_type=MESH)
    pl.semaphore_wait(barrier, len(peers))


def deal_kernel(order, hidden, full, *scratch):
    held = scratch[:CHUNKS]
    far_out, far_in, near_out, near_in = scratch[CHUNKS:CHUNKS + 4]
    (load_sem, z_send, z_recv, far_send, far_recv, near_send, near_recv,
     y_send, y_recv, half_send, half_recv, sib_send, sib_recv) = scratch[CHUNKS + 4:]
    req, tp, z, x, y, c = place()

    def at_z(step):
        return lax.rem(z + step + NZ, NZ) * NX + x

    def at_x(step):
        return z * NX + lax.rem(x + step + NX, NX)

    def at_y(step):
        return lax.rem(y + step + NY, NY) * 2 + c

    sign = (1, -1)
    sibling = y * 2 + 1 - c

    loads = [
        pltpu.make_async_copy(
            hidden.at[:, pl.ds(STARTS[k], SIZES[k]), :], held[k].at[pl.ds(z * SLOTS, SLOTS)], load_sem.at[k]
        )
        for k in range(CHUNKS)
    ]
    for load in loads:
        load.start()
    greet([(at_z(1), tp), (at_z(-1), tp), (at_x(1), tp), (at_x(-1), tp),
           (req, at_y(1)), (req, at_y(-1)), (req, sibling)])

    def z_copy(k, hop, d, arriving):
        back = hop if arriving else hop - 1
        owner = lax.rem(z - sign[d] * back + 2 * NZ, NZ)
        count = SLOTS if hop < 4 else SLOTS // 2
        first = 0 if hop < 4 or d == 0 else SLOTS // 2
        block = held[k].at[pl.ds(owner * SLOTS + first, count)]
        return remote(block, block, z_send.at[d, hop - 1, k], z_recv.at[d, hop - 1, k], at_z(sign[d]), tp)

    def rows(k):
        return pl.ds(STARTS[k], SIZES[k])

    def far_copy(k, d):
        return remote(far_out.at[d, :, rows(k)], far_in.at[d, :, rows(k)],
                      far_send.at[d, k], far_recv.at[d, k], at_x(sign[d]), tp)

    def near_copy(k, d):
        return remote(near_out.at[d, :, rows(k)], near_in.at[d, :, rows(k)],
                      near_send.at[d, k], near_recv.at[d, k], at_x(sign[d]), tp)

    def y_copy(k, d, arriving):
        piece = full.at[at_y(-sign[d]) if arriving else tp, :, rows(k)]
        return remote(piece, piece, y_send.at[d, k], y_recv.at[d, k], req, at_y(sign[d]))

    def half_copy(k, d, arriving):
        owner = at_y(-2 * sign[d]) if arriving else at_y(-sign[d])
        piece = full.at[owner, pl.ds(d * SLOTS // 2, SLOTS // 2), rows(k)]
        return remote(piece, piece, half_send.at[d, k], half_recv.at[d, k], req, at_y(sign[d]))

    def sib_copy(k, part, arriving):
        core = 1 - c if arriving else c
        step = (0, -1, 1, 2)[part]
        piece = full.at[lax.rem(y + step + NY, NY) * 2 + core, :, rows(k)]
        return remote(piece, piece, sib_send.at[part, k], sib_recv.at[part, k], req, sibling)

    def source(step, j):
        request = order[at_x(step) * SLOTS + j]
        device = request // SLOTS
        return (device // NX) * SLOTS + request % SLOTS, device % NX

    source = functools.lru_cache(None)(source)

    def z_send_step(k, hop):
        for d in (0, 1):
            if hop == 1:
                if d == 0:
                    loads[k].wait()
            else:
                z_copy(k, hop - 1, d, True).wait_recv()
            z_copy(k, hop, d, False).start()

    def x_far(k):
        for d in (0, 1):
            z_copy(k, 4, d, True).wait_recv()
        for d in (0, 1):
            for i in range(SLOTS // 2):
                j = i + d * SLOTS // 2
                far_out[d, i, rows(k)] = held[k][source(2, j)[0]]
            far_copy(k, d).start()

    def x_near(k):
        for d in (0, 1):
            far_copy(k, d).wait_recv()
            for j in range(SLOTS):
                index, column = source(sign[d], j)
                mine = held[k][index]
                i = j - d * SLOTS // 2
                if 0 <= i < SLOTS // 2:
                    mine = lax.select(column == x, mine, far_in[d, i, rows(k)])
                near_out[d, j, rows(k)] = mine
            near_copy(k, d).start()

    def x_done(k):
        for d in (0, 1):
            near_copy(k, d).wait_recv()
        for j in range(SLOTS):
            index, column = source(0, j)
            offset = lax.rem(column - x + NX, NX)
            if j < SLOTS // 2:
                from_left = offset >= 2
            else:
                from_left = offset == 3
            mine = held[k][index]
            other = lax.select(from_left, near_in[0, j, rows(k)], near_in[1, j, rows(k)])
            full[tp, j, rows(k)] = lax.select(offset == 0, mine, other)
        for d in (0, 1):
            y_copy(k, d, False).start()
        sib_copy(k, 0, False).start()

    def y_forward(k):
        for d in (0, 1):
            y_copy(k, d, True).wait_recv()
            half_copy(k, d, False).start()
            sib_copy(k, 1 + d, False).start()

    def y_finish(k):
        for d in (0, 1):
            half_copy(k, d, True).wait_recv()
        sib_copy(k, 3, False).start()

    stages = (None, *(functools.partial(z_send_step, hop=hop) for hop in (1, 2, 3, 4)),
              x_far, x_near, x_done, y_forward, y_finish)
    for mark in ORDER:
        stages[mark % 10](mark // 10)

    for k in range(CHUNKS):
        for part in range(4):
            sib_copy(k, part, True).wait_recv()
    for k in range(CHUNKS):
        for d in (0, 1):
            for hop in (1, 2, 3, 4):
                z_copy(k, hop, d, False).wait_send()
            far_copy(k, d).wait_send()
            near_copy(k, d).wait_send()
            y_copy(k, d, False).wait_send()
            half_copy(k, d, False).wait_send()
        for part in range(4):
            sib_copy(k, part, False).wait_send()


def deal(order, hidden):
    dma = pltpu.SemaphoreType.DMA
    return pl.pallas_call(
        deal_kernel,
        out_shape=jax.ShapeDtypeStruct((TP, SLOTS, NODES, WIDTH), jnp.bfloat16),
        in_specs=[pl.BlockSpec(memory_space=pltpu.SMEM), pl.BlockSpec(memory_space=pl.ANY)],
        out_specs=pl.BlockSpec(memory_space=pltpu.VMEM),
        scratch_shapes=[pltpu.VMEM((NZ * SLOTS, size, WIDTH), jnp.bfloat16) for size in SIZES] + [
            pltpu.VMEM((2, SLOTS // 2, NODES, WIDTH), jnp.bfloat16),
            pltpu.VMEM((2, SLOTS // 2, NODES, WIDTH), jnp.bfloat16),
            pltpu.VMEM((2, SLOTS, NODES, WIDTH), jnp.bfloat16),
            pltpu.VMEM((2, SLOTS, NODES, WIDTH), jnp.bfloat16),
            dma((CHUNKS,)),
            dma((2, 4, CHUNKS)), dma((2, 4, CHUNKS)),
            dma((2, CHUNKS)), dma((2, CHUNKS)),
            dma((2, CHUNKS)), dma((2, CHUNKS)),
            dma((2, CHUNKS)), dma((2, CHUNKS)),
            dma((2, CHUNKS)), dma((2, CHUNKS)),
            dma((4, CHUNKS)), dma((4, CHUNKS)),
        ],
        compiler_params=pltpu.CompilerParams(
            collective_id=0, has_side_effects=True, vmem_limit_bytes=24 * 2**20
        ),
        name="deal",
    )(order, hidden)


def tree_kernel(lengths, parents, freq, ancestry, cosine, sine):
    low = lax.broadcasted_iota(jnp.int32, (NODES, NODES), 0)
    high = lax.broadcasted_iota(jnp.int32, (NODES, NODES), 1)
    eye = (low == high).astype(jnp.float32)
    lane = lax.broadcasted_iota(jnp.int32, (NODES, HEAD), 1)
    links = []
    for s in range(SLOTS):
        link = ((low == parents[s:s + 1, :]) & (high > 0)).astype(jnp.float32)
        links.append(jnp.minimum(eye + link, 1.0))
    for _ in range((NODES - 1).bit_length()):
        links = [
            jnp.minimum(
                jnp.dot(a.astype(jnp.bfloat16), a.astype(jnp.bfloat16), preferred_element_type=jnp.float32), 1.0
            )
            for a in links
        ]
    for s in range(SLOTS):
        above = links[s].T
        ancestry[s] = above
        depth = jnp.sum(above, axis=-1, keepdims=True)
        position = lengths[s].astype(jnp.float32) + depth - 1.0
        angle = position * freq[...]
        cosine[s] = jnp.cos(angle)
        turned = jnp.sin(angle)
        sine[s] = jnp.where(lane < HEAD // 2, -turned, turned)


def tree(lengths, parents):
    half = HEAD // 2
    freq = 500000.0 ** (-2.0 * np.arange(half, dtype=np.float64) / HEAD)
    freq = jnp.asarray(np.concatenate([freq, freq])[None].astype(np.float32))
    vmem = pl.BlockSpec(memory_space=pltpu.VMEM)
    return pl.pallas_call(
        tree_kernel,
        out_shape=(
            jax.ShapeDtypeStruct((SLOTS, NODES, NODES), jnp.float32),
            jax.ShapeDtypeStruct((SLOTS, NODES, HEAD), jnp.float32),
            jax.ShapeDtypeStruct((SLOTS, NODES, HEAD), jnp.float32),
        ),
        in_specs=[pl.BlockSpec(memory_space=pltpu.SMEM), vmem, vmem],
        out_specs=(vmem, vmem, vmem),
        name="tree",
    )(lengths, parents, freq)


GROUPS = ((0, 2), (2, 4), (4, 5), (5, 6))


def finish_kernel(lengths, kept, full, gain, ancestry, cosine, sine, w_query, w_key, w_value, w_out, key_cache,
                  value_cache, out, appended, normed, wq, wk, wv, wo, keys, values, q_rows, kv_rows, q_rot, fresh_k,
                  fresh_v, raw, attended, *scratch):
    count = len(GROUPS)
    sib_out, sib_in, own, far_out, far_in, near_out, near_in = (
        scratch[i * count:(i + 1) * count] for i in range(7)
    )
    w_sem, kv_sem, sib_send, sib_recv, far_send, far_recv, near_send, near_recv = scratch[7 * count:]
    req, tp, z, x, y, c = place()
    sign = (1, -1)
    sibling = y * 2 + 1 - c

    def at_y(step):
        return lax.rem(y + step + NY, NY) * 2 + c

    loads = [
        pltpu.make_async_copy(src, dst, w_sem.at[i])
        for i, (src, dst) in enumerate(((w_query, wq), (w_key, wk), (w_value, wv), (w_out, wo)))
    ]
    for load in loads:
        load.start()

    def cache_loads(s):
        return (
            pltpu.make_async_copy(key_cache.at[s], keys.at[s], kv_sem.at[0, s]),
            pltpu.make_async_copy(value_cache.at[s], values.at[s], kv_sem.at[1, s]),
        )

    for s in range(SLOTS):
        for load in cache_loads(s):
            load.start()

    greet([(req, at_y(1)), (req, at_y(-1)), (req, sibling)])

    rows = SLOTS * NODES
    step = 128
    for r in range(0, rows, step):
        pieces = [full[t, r:r + step, :].astype(jnp.float32) for t in range(TP)]
        total = sum(jnp.sum(p * p, axis=-1, keepdims=True) for p in pieces)
        inverse = lax.rsqrt(total * (1.0 / (TP * WIDTH)) + EPS)
        for t in range(TP):
            scaled = pieces[t] * inverse * gain[:, t * WIDTH:(t + 1) * WIDTH].astype(jnp.float32)
            normed[r:r + step, t * WIDTH:(t + 1) * WIDTH] = scaled.astype(jnp.bfloat16)
    for load in loads[:3]:
        load.wait()
    q_rows[...] = jnp.dot(normed[...], wq[...], preferred_element_type=jnp.float32)
    kv_rows[:, :HEAD] = jnp.dot(normed[...], wk[...], preferred_element_type=jnp.float32)
    kv_rows[:, HEAD:] = jnp.dot(normed[...], wv[...], preferred_element_type=jnp.float32)

    kept_lane = lax.broadcasted_iota(jnp.int32, (KEEP, NODES), 1)
    kept_row = lax.broadcasted_iota(jnp.int32, (KEEP, NODES), 0)
    block_lane = lax.broadcasted_iota(jnp.int32, (1, BLOCK), 1)
    factor = SCALE * LOG2E
    transposed = (((1,), (1,)), ((), ()))

    for s in range(SLOTS):
        node_rows = slice(s * NODES, (s + 1) * NODES)
        co, si = cosine[s], sine[s]

        def rotated(u):
            return (u * co + pltpu.roll(u, HEAD // 2, 1) * si).astype(jnp.bfloat16)

        key = rotated(kv_rows[node_rows, :HEAD])
        value = kv_rows[node_rows, HEAD:].astype(jnp.bfloat16)
        fresh_k[s] = key
        fresh_v[s] = value
        select = kept_row * 0 + kept[s, 0]
        for k in range(1, KEEP):
            select = jnp.where(kept_row == k, kept[s, k], select)
        onehot = (select == kept_lane).astype(jnp.bfloat16)
        appended[s, 0] = jnp.dot(onehot, key, preferred_element_type=jnp.float32).astype(jnp.bfloat16)
        appended[s, 1] = jnp.dot(onehot, value, preferred_element_type=jnp.float32).astype(jnp.bfloat16)
        for h in range(3):
            q_rot[s, h * NODES:(h + 1) * NODES, :] = rotated(q_rows[node_rows, h * HEAD:(h + 1) * HEAD])

    def slot(s, length, count):
        query = q_rot[s]
        visible = ancestry[s] > 0
        tree_scores = lax.dot_general(query, fresh_k[s], transposed, preferred_element_type=jnp.float32)
        tree_scores = jnp.concatenate(
            [
                jnp.where(visible, tree_scores[h * NODES:(h + 1) * NODES], -jnp.inf)
                for h in range(3)
            ],
            axis=0,
        )
        best = None
        for b in range(count):
            sc = lax.dot_general(
                query, keys[s, b * BLOCK:(b + 1) * BLOCK, :], transposed, preferred_element_type=jnp.float32
            )
            if b >= SHORTEST - 1:
                sc = jnp.where(block_lane < length - b * BLOCK, sc, -jnp.inf)
            raw[b] = sc
            for i in range(BLOCK // HEAD):
                part = sc[:, i * HEAD:(i + 1) * HEAD]
                best = part if best is None else jnp.maximum(best, part)
        top = jnp.maximum(
            jnp.max(tree_scores, axis=-1, keepdims=True), jnp.max(best, axis=-1, keepdims=True)
        ) * factor
        weight = jnp.exp2(tree_scores * factor - top)
        small = jnp.sum(weight, axis=-1, keepdims=True)
        acc = jnp.dot(weight.astype(jnp.bfloat16), fresh_v[s], preferred_element_type=jnp.float32)
        total = None
        for b in range(count):
            p = jnp.exp2(raw[b] * factor - top)
            for i in range(BLOCK // HEAD):
                part = p[:, i * HEAD:(i + 1) * HEAD]
                total = part if total is None else total + part
            acc = acc + jnp.dot(
                p.astype(jnp.bfloat16), values[s, b * BLOCK:(b + 1) * BLOCK, :], preferred_element_type=jnp.float32
            )
        small = small + jnp.sum(total, axis=-1, keepdims=True)
        result = (acc / small).astype(jnp.bfloat16)
        node_rows = pl.ds(pl.multiple_of(s * NODES, NODES), NODES)
        for h in range(3):
            attended[node_rows, h * HEAD:(h + 1) * HEAD] = result[h * NODES:(h + 1) * NODES]

    def group_rows(r):
        lo, hi = GROUPS[r]
        return slice(lo * NODES, hi * NODES)

    def term(r, step, core):
        target = lax.rem(y + step + NY, NY) * 2 + core
        columns = pl.ds(pl.multiple_of(target * WIDTH, 128), WIDTH)
        return jnp.dot(attended[group_rows(r), :], wo[:, columns], preferred_element_type=jnp.float32)

    def sib_copy(r, i):
        return remote(sib_out[r].at[i], sib_in[r].at[i], sib_send.at[r, i], sib_recv.at[r, i], req, sibling)

    def far_copy(r, d):
        return remote(far_out[r].at[d], far_in[r].at[d], far_send.at[r, d], far_recv.at[r, d], req, at_y(sign[d]))

    def near_copy(r, d):
        return remote(near_out[r].at[d], near_in[r].at[d], near_send.at[r, d], near_recv.at[r, d], req, at_y(sign[d]))

    steps = (2, 1, -1, 0)

    def first(r):
        for i, step in enumerate(steps):
            sib_out[r][i] = term(r, step, 1 - c).astype(jnp.bfloat16)
            sib_copy(r, i).start()
        for i, step in enumerate(steps):
            own[r][i] = term(r, step, c)

    def pair(r, i):
        sib_copy(r, i).wait_recv()
        return own[r][i] + sib_in[r][i].astype(jnp.float32)

    def far(r):
        both = pair(r, 0).astype(jnp.bfloat16)
        half = both.shape[0] // 2
        for d in (0, 1):
            far_out[r][d] = both[d * half:(d + 1) * half]
            far_copy(r, d).start()

    def near(r):
        for d in (0, 1):
            mine = pair(r, 1 + d)
            far_copy(r, d).wait_recv()
            half = mine.shape[0] // 2
            lo, hi = d * half, (d + 1) * half
            rest = slice(half, 2 * half) if d == 0 else slice(0, half)
            near_out[r][d, lo:hi] = (mine[lo:hi] + far_in[r][d].astype(jnp.float32)).astype(jnp.bfloat16)
            near_out[r][d, rest] = mine[rest].astype(jnp.bfloat16)
            near_copy(r, d).start()

    def last(r):
        mine = pair(r, 3) + full[tp, group_rows(r), :].astype(jnp.float32)
        for d in (0, 1):
            near_copy(r, d).wait_recv()
            mine = mine + near_in[r][d].astype(jnp.float32)
        out[group_rows(r), :] = mine.astype(jnp.bfloat16)

    def attention(r):
        @pl.loop(*GROUPS[r])
        def _(s):
            for load in cache_loads(s):
                load.wait()
            slot(s, lengths[s], CACHE // BLOCK)

    attention(0)
    loads[3].wait()
    first(0)
    attention(1)
    far(0)
    first(1)
    attention(2)
    far(1)
    first(2)
    near(0)
    attention(3)
    far(2)
    first(3)
    near(1)
    last(0)
    far(3)
    near(2)
    last(1)
    near(3)
    last(2)
    last(3)
    for r in range(count):
        for i in range(4):
            sib_copy(r, i).wait_send()
        for d in (0, 1):
            far_copy(r, d).wait_send()
            near_copy(r, d).wait_send()


def finish(lengths, kept, full, gain, tables, w_query, w_key, w_value, w_out, key_cache, value_cache):
    vmem = pl.BlockSpec(memory_space=pltpu.VMEM)
    smem = pl.BlockSpec(memory_space=pltpu.SMEM)
    hbm = pl.BlockSpec(memory_space=pl.ANY)
    rows = SLOTS * NODES
    bf16, f32 = jnp.bfloat16, jnp.float32
    model = TP * WIDTH
    dma = pltpu.SemaphoreType.DMA
    sizes = [(hi - lo) * NODES for lo, hi in GROUPS]
    exchanged = (
        [pltpu.VMEM((4, n, WIDTH), bf16) for n in sizes] * 2
        + [pltpu.VMEM((4, n, WIDTH), f32) for n in sizes]
        + [pltpu.VMEM((2, n // 2, WIDTH), bf16) for n in sizes] * 2
        + [pltpu.VMEM((2, n, WIDTH), bf16) for n in sizes] * 2
    )
    count = len(GROUPS)
    return pl.pallas_call(
        finish_kernel,
        out_shape=(
            jax.ShapeDtypeStruct((rows, WIDTH), bf16),
            jax.ShapeDtypeStruct((SLOTS, 2, KEEP, HEAD), bf16),
        ),
        in_specs=[smem, smem, vmem, vmem, vmem, vmem, vmem] + [hbm] * 6,
        out_specs=(vmem, vmem),
        scratch_shapes=[
            pltpu.VMEM((rows, model), bf16),
            pltpu.VMEM((model, WIDTH), bf16),
            pltpu.VMEM((model, HEAD), bf16),
            pltpu.VMEM((model, HEAD), bf16),
            pltpu.VMEM((WIDTH, model), bf16),
            pltpu.VMEM((SLOTS, CACHE, HEAD), bf16),
            pltpu.VMEM((SLOTS, CACHE, HEAD), bf16),
            pltpu.VMEM((rows, WIDTH), f32),
            pltpu.VMEM((rows, 2 * HEAD), f32),
            pltpu.VMEM((SLOTS, 3 * NODES, HEAD), bf16),
            pltpu.VMEM((SLOTS, NODES, HEAD), bf16),
            pltpu.VMEM((SLOTS, NODES, HEAD), bf16),
            pltpu.VMEM((CACHE // BLOCK, 3 * NODES, BLOCK), f32),
            pltpu.VMEM((rows, WIDTH), bf16),
            *exchanged,
            dma((4,)), dma((2, SLOTS)),
            dma((count, 4)), dma((count, 4)),
            dma((count, 2)), dma((count, 2)),
            dma((count, 2)), dma((count, 2)),
        ],
        compiler_params=pltpu.CompilerParams(
            collective_id=1, has_side_effects=True, vmem_limit_bytes=52 * 2**20
        ),
        name="finish",
    )(lengths, kept, full, gain, *tables, w_query, w_key, w_value, w_out, key_cache, value_cache)


def body(hidden_in, request_order, norm_gain, w_query, key_weight, value_weight, w_out,
         key_cache, cached_values, cache_lengths, tree_parent, kept_nodes):
    rows = SLOTS * NODES
    tables = tree(cache_lengths, tree_parent)
    full = deal(request_order, hidden_in).reshape(TP, rows, WIDTH)
    layer_out, appended = finish(
        cache_lengths, kept_nodes, full, norm_gain.reshape(1, -1), tables, w_query, key_weight, value_weight, w_out,
        key_cache.reshape(SLOTS, CACHE, HEAD), cached_values.reshape(SLOTS, CACHE, HEAD),
    )
    return layer_out.reshape(SLOTS, NODES, WIDTH), appended.reshape(SLOTS, 2, KEEP, 1, HEAD)


def solution(mesh):
    placed = (
        P("req", None, "tp"), P(), P(), P(None, "tp"), P(None, "tp"), P(None, "tp"), P("tp", None),
        P("req", "tp", None, None), P("req", "tp", None, None), P("req"), P("req", None), P("req", None),
    )
    return jax.shard_map(
        body,
        mesh=mesh,
        in_specs=placed,
        out_specs=(P("req", None, "tp"), P("req", None, None, "tp", None)),
        check_vma=False,
    )
```

```python
import functools
import math

import jax
import jax.numpy as jnp
import numpy as np
from jax import lax
from jax.experimental import pallas as pl
from jax.experimental.pallas import tpu as pltpu
from jax.sharding import PartitionSpec as P

MESH = pl.DeviceIdType.MESH
HEAD = 128
EPS = 1e-05
SLOTS, NODES, WIDTH = 6, 64, 384
NX, NZ, NY = 4, 8, 4
TP = 8
CACHE = 3456
KEEP = 8
SIZES = (16, 16, 16, 16)
STARTS = (0, 16, 32, 48)
CHUNKS = len(SIZES)
ORDER = (
    1, 11, 2, 12, 3, 13, 4, 21, 31, -1, 14, 5, 22, 32, 6, 15, 23, 33, 16, 24,
    7, 34, 25, 17, 35, 8, 26, 36, 9, 18, 27, 19, 37, 28, 0, 38, 29, 10, 39, 20,
    30,
)
GROUPS = ((0, 2), (2, 4), (4, 5), (5, 6))
BLOCK = 384
SHORTEST = 3
LOG2E = math.log2(math.e)
SCALE = HEAD ** (-0.5)


def remote(src, dst, send, recv, req, tp):
    return pltpu.make_async_remote_copy(
        src_ref=src, dst_ref=dst, send_sem=send, recv_sem=recv,
        device_id=(req, tp), device_id_type=MESH,
    )


def place():
    req = lax.axis_index("req")
    tp = lax.axis_index("tp")
    return req, tp, req // NX, req % NX, tp // 2, tp % 2


def greet(peers):
    barrier = pltpu.get_barrier_semaphore()
    for req, tp in peers:
        pl.semaphore_signal(barrier, inc=1, device_id=(req, tp), device_id_type=MESH)
    pl.semaphore_wait(barrier, len(peers))


def layer_kernel(order_hbm, lengths_hbm, kept_hbm, parents_hbm, freq_hbm, hidden, gain, w_query, w_key, w_value, w_out,
                 key_cache, value_cache, out, appended, order, lengths, kept, parents, freq, full, ancestry, cosine, sine,
                 normed, wq, wk, wv, wo, keys, values, q_rot, fresh_k, fresh_v, raw, attended,
                 far_out, far_in, near_out, near_in, load_sem, small_sem, z_send, z_recv, far_send, far_recv, near_send,
                 near_recv, y_send, y_recv, half_send, half_recv, core_send, core_recv, w_sem, kv_sem, sum_send, sum_recv,
                 out_far_send, out_far_recv, out_near_send, out_near_recv, *scratch):
    held = scratch[:CHUNKS]
    count = len(GROUPS)
    sib_out, sib_in, own, sum_far_out, sum_far_in, sum_near_out, sum_near_in = (
        scratch[CHUNKS + i * count:CHUNKS + (i + 1) * count] for i in range(7)
    )
    req, tp, z, x, y, c = place()

    def at_z(step):
        return lax.rem(z + step + NZ, NZ) * NX + x

    def at_x(step):
        return z * NX + lax.rem(x + step + NX, NX)

    def at_y(step):
        return lax.rem(y + step + NY, NY) * 2 + c

    sign = (1, -1)
    sibling = y * 2 + 1 - c

    deals = [
        pltpu.make_async_copy(
            hidden.at[:, pl.ds(STARTS[k], SIZES[k]), :], held[k].at[pl.ds(z * SLOTS, SLOTS)], load_sem.at[k]
        )
        for k in range(CHUNKS)
    ]
    smalls = [
        pltpu.make_async_copy(src, dst, small_sem.at[i])
        for i, (src, dst) in enumerate((
            (order_hbm, order), (lengths_hbm, lengths), (kept_hbm, kept), (parents_hbm, parents), (freq_hbm, freq)
        ))
    ]
    loads = [
        pltpu.make_async_copy(src, dst, w_sem.at[i])
        for i, (src, dst) in enumerate(((w_query, wq), (w_key, wk), (w_value, wv), (w_out, wo)))
    ]

    def cache_loads(s):
        return (
            pltpu.make_async_copy(key_cache.at[s], keys.at[s], kv_sem.at[0, s]),
            pltpu.make_async_copy(value_cache.at[s], values.at[s], kv_sem.at[1, s]),
        )

    for load in deals + smalls:
        load.start()
    greet([(at_z(1), tp), (at_z(-1), tp), (at_x(1), tp), (at_x(-1), tp),
           (req, at_y(1)), (req, at_y(-1)), (req, sibling)])

    def z_copy(k, hop, d, arriving):
        back = hop if arriving else hop - 1
        owner = lax.rem(z - sign[d] * back + 2 * NZ, NZ)
        count = SLOTS if hop < 4 else SLOTS // 2
        first = 0 if hop < 4 or d == 0 else SLOTS // 2
        block = held[k].at[pl.ds(owner * SLOTS + first, count)]
        return remote(block, block, z_send.at[d, hop - 1, k], z_recv.at[d, hop - 1, k], at_z(sign[d]), tp)

    def rows(k):
        return pl.ds(STARTS[k], SIZES[k])

    def far_copy(k, d):
        return remote(far_out.at[d, :, rows(k)], far_in.at[d, :, rows(k)],
                      far_send.at[d, k], far_recv.at[d, k], at_x(sign[d]), tp)

    def near_copy(k, d):
        return remote(near_out.at[d, :, rows(k)], near_in.at[d, :, rows(k)],
                      near_send.at[d, k], near_recv.at[d, k], at_x(sign[d]), tp)

    def y_copy(k, d, arriving):
        piece = full.at[at_y(-sign[d]) if arriving else tp, :, rows(k)]
        return remote(piece, piece, y_send.at[d, k], y_recv.at[d, k], req, at_y(sign[d]))

    def half_copy(k, d, arriving):
        owner = at_y(-2 * sign[d]) if arriving else at_y(-sign[d])
        piece = full.at[owner, pl.ds(d * SLOTS // 2, SLOTS // 2), rows(k)]
        return remote(piece, piece, half_send.at[d, k], half_recv.at[d, k], req, at_y(sign[d]))

    def core_copy(k, part, arriving):
        core = 1 - c if arriving else c
        step = (0, -1, 1, 2)[part]
        piece = full.at[lax.rem(y + step + NY, NY) * 2 + core, :, rows(k)]
        return remote(piece, piece, core_send.at[part, k], core_recv.at[part, k], req, sibling)

    def source(step, j):
        request = order[at_x(step) * SLOTS + j]
        device = request // SLOTS
        return (device // NX) * SLOTS + request % SLOTS, device % NX

    source = functools.lru_cache(None)(source)

    def z_send_step(k, hop):
        for d in (0, 1):
            if hop == 1:
                if d == 0:
                    deals[k].wait()
            else:
                z_copy(k, hop - 1, d, True).wait_recv()
            z_copy(k, hop, d, False).start()

    def x_far(k):
        for d in (0, 1):
            z_copy(k, 4, d, True).wait_recv()
        for d in (0, 1):
            for i in range(SLOTS // 2):
                j = i + d * SLOTS // 2
                far_out[d, i, rows(k)] = held[k][source(2, j)[0]]
            far_copy(k, d).start()

    def x_near(k):
        for d in (0, 1):
            far_copy(k, d).wait_recv()
            for j in range(SLOTS):
                index, column = source(sign[d], j)
                mine = held[k][index]
                i = j - d * SLOTS // 2
                if 0 <= i < SLOTS // 2:
                    mine = lax.select(column == x, mine, far_in[d, i, rows(k)])
                near_out[d, j, rows(k)] = mine
            near_copy(k, d).start()

    def x_done(k):
        for d in (0, 1):
            near_copy(k, d).wait_recv()
        for j in range(SLOTS):
            index, column = source(0, j)
            offset = lax.rem(column - x + NX, NX)
            if j < SLOTS // 2:
                from_left = offset >= 2
            else:
                from_left = offset == 3
            mine = held[k][index]
            other = lax.select(from_left, near_in[0, j, rows(k)], near_in[1, j, rows(k)])
            full[tp, j, rows(k)] = lax.select(offset == 0, mine, other)
        for d in (0, 1):
            y_copy(k, d, False).start()
        core_copy(k, 0, False).start()

    def y_forward(k):
        for d in (0, 1):
            y_copy(k, d, True).wait_recv()
            half_copy(k, d, False).start()
            core_copy(k, 1 + d, False).start()

    def y_finish(k):
        for d in (0, 1):
            half_copy(k, d, True).wait_recv()
        core_copy(k, 3, False).start()

    def trees():
        for load in smalls:
            load.wait()
        for load in loads:
            load.start()
        for s in range(SLOTS):
            for load in cache_loads(s):
                load.start()
        low = lax.broadcasted_iota(jnp.int32, (NODES, NODES), 0)
        high = lax.broadcasted_iota(jnp.int32, (NODES, NODES), 1)
        eye = (low == high).astype(jnp.float32)
        lane = lax.broadcasted_iota(jnp.int32, (NODES, HEAD), 1)
        links = []
        for s in range(SLOTS):
            link = ((low == parents[s:s + 1, :]) & (high > 0)).astype(jnp.float32)
            links.append(jnp.minimum(eye + link, 1.0))
        for _ in range((NODES - 1).bit_length()):
            links = [
                jnp.minimum(
                    jnp.dot(a.astype(jnp.bfloat16), a.astype(jnp.bfloat16), preferred_element_type=jnp.float32), 1.0
                )
                for a in links
            ]
        for s in range(SLOTS):
            above = links[s].T
            ancestry[s] = above
            depth = jnp.sum(above, axis=-1, keepdims=True)
            position = lengths[s].astype(jnp.float32) + depth - 1.0
            angle = position * freq[...]
            cosine[s] = jnp.cos(angle)
            turned = jnp.sin(angle)
            sine[s] = jnp.where(lane < HEAD // 2, -turned, turned)

    factor = SCALE * LOG2E
    transposed = (((1,), (1,)), ((), ()))
    block_lane = lax.broadcasted_iota(jnp.int32, (1, BLOCK), 1)

    def chunk_project(k):
        if k == 0:
            for load in loads[:3]:
                load.wait()
        for part in range(4):
            core_copy(k, part, True).wait_recv()
        size = SIZES[k]
        piece_rows = SLOTS * size
        pieces = [full[t, :, rows(k)].astype(jnp.float32).reshape(piece_rows, WIDTH) for t in range(TP)]
        total = sum(jnp.sum(p * p, axis=-1, keepdims=True) for p in pieces)
        inverse = lax.rsqrt(total * (1.0 / (TP * WIDTH)) + EPS)
        span = slice(SLOTS * STARTS[k], SLOTS * STARTS[k] + piece_rows)
        for t in range(TP):
            scaled = pieces[t] * inverse * gain[:, t * WIDTH:(t + 1) * WIDTH].astype(jnp.float32)
            normed[span, t * WIDTH:(t + 1) * WIDTH] = scaled.astype(jnp.bfloat16)
        table = normed[span, :]
        query = jnp.dot(table, wq[...], preferred_element_type=jnp.float32)
        new_keys = jnp.dot(table, wk[...], preferred_element_type=jnp.float32)
        new_values = jnp.dot(table, wv[...], preferred_element_type=jnp.float32)
        for s in range(SLOTS):
            lo, hi = s * size, (s + 1) * size
            co, si = cosine[s, rows(k)], sine[s, rows(k)]

            def rotated(u):
                return (u * co + pltpu.roll(u, HEAD // 2, 1) * si).astype(jnp.bfloat16)

            fresh_k[s, rows(k)] = rotated(new_keys[lo:hi])
            fresh_v[s, rows(k)] = new_values[lo:hi].astype(jnp.bfloat16)
            for h in range(3):
                q_rot[s, h * NODES + STARTS[k]:h * NODES + STARTS[k] + size, :] = rotated(
                    query[lo:hi, h * HEAD:(h + 1) * HEAD]
                )

    stages = (chunk_project, *(functools.partial(z_send_step, hop=hop) for hop in (1, 2, 3, 4)),
              x_far, x_near, x_done, y_forward, y_finish)
    for mark in ORDER:
        if mark < 0:
            trees()
        else:
            stages[mark % 10](mark // 10)

    def append(s):
        kept_lane = lax.broadcasted_iota(jnp.int32, (KEEP, NODES), 1)
        kept_row = lax.broadcasted_iota(jnp.int32, (KEEP, NODES), 0)
        select = kept_row * 0 + kept[s, 0]
        for k in range(1, KEEP):
            select = jnp.where(kept_row == k, kept[s, k], select)
        onehot = (select == kept_lane).astype(jnp.bfloat16)
        for i, source_rows in enumerate((fresh_k[s], fresh_v[s])):
            appended[s, i] = jnp.dot(onehot, source_rows, preferred_element_type=jnp.float32).astype(jnp.bfloat16)

    def slot(s, length, blocks):
        query = q_rot[s]
        visible = ancestry[s] > 0
        tree_scores = lax.dot_general(query, fresh_k[s], transposed, preferred_element_type=jnp.float32)
        tree_scores = jnp.concatenate(
            [
                jnp.where(visible, tree_scores[h * NODES:(h + 1) * NODES], -jnp.inf)
                for h in range(3)
            ],
            axis=0,
        )
        best = None
        for b in range(blocks):
            sc = lax.dot_general(
                query, keys[s, b * BLOCK:(b + 1) * BLOCK, :], transposed, preferred_element_type=jnp.float32
            )
            if b >= SHORTEST - 1:
                sc = jnp.where(block_lane < length - b * BLOCK, sc, -jnp.inf)
            raw[b] = sc
            for i in range(BLOCK // HEAD):
                part = sc[:, i * HEAD:(i + 1) * HEAD]
                best = part if best is None else jnp.maximum(best, part)
        top = jnp.maximum(
            jnp.max(tree_scores, axis=-1, keepdims=True), jnp.max(best, axis=-1, keepdims=True)
        ) * factor
        weight = jnp.exp2(tree_scores * factor - top)
        small = jnp.sum(weight, axis=-1, keepdims=True)
        acc = jnp.dot(weight.astype(jnp.bfloat16), fresh_v[s], preferred_element_type=jnp.float32)
        total = None
        for b in range(blocks):
            p = jnp.exp2(raw[b] * factor - top)
            for i in range(BLOCK // HEAD):
                part = p[:, i * HEAD:(i + 1) * HEAD]
                total = part if total is None else total + part
            acc = acc + jnp.dot(
                p.astype(jnp.bfloat16), values[s, b * BLOCK:(b + 1) * BLOCK, :], preferred_element_type=jnp.float32
            )
        small = small + jnp.sum(total, axis=-1, keepdims=True)
        result = (acc / small).astype(jnp.bfloat16)
        node_rows = pl.ds(pl.multiple_of(s * NODES, NODES), NODES)
        for h in range(3):
            attended[node_rows, h * HEAD:(h + 1) * HEAD] = result[h * NODES:(h + 1) * NODES]

    def group_rows(r):
        lo, hi = GROUPS[r]
        return slice(lo * NODES, hi * NODES)

    def term(r, step, core):
        target = lax.rem(y + step + NY, NY) * 2 + core
        columns = pl.ds(pl.multiple_of(target * WIDTH, 128), WIDTH)
        return jnp.dot(attended[group_rows(r), :], wo[:, columns], preferred_element_type=jnp.float32)

    def sib_copy(r, i):
        return remote(sib_out[r].at[i], sib_in[r].at[i], sum_send.at[r, i], sum_recv.at[r, i], req, sibling)

    def out_far_copy(r, d):
        return remote(sum_far_out[r].at[d], sum_far_in[r].at[d], out_far_send.at[r, d], out_far_recv.at[r, d], req, at_y(sign[d]))

    def out_near_copy(r, d):
        return remote(sum_near_out[r].at[d], sum_near_in[r].at[d], out_near_send.at[r, d], out_near_recv.at[r, d], req, at_y(sign[d]))

    steps = (2, 1, -1, 0)

    def first(r):
        for i, step in enumerate(steps):
            sib_out[r][i] = term(r, step, 1 - c).astype(jnp.bfloat16)
            sib_copy(r, i).start()
        for i, step in enumerate(steps):
            own[r][i] = term(r, step, c)

    def pair(r, i):
        sib_copy(r, i).wait_recv()
        return own[r][i] + sib_in[r][i].astype(jnp.float32)

    def far(r):
        both = pair(r, 0).astype(jnp.bfloat16)
        half = both.shape[0] // 2
        for d in (0, 1):
            sum_far_out[r][d] = both[d * half:(d + 1) * half]
            out_far_copy(r, d).start()

    def near(r):
        for d in (0, 1):
            mine = pair(r, 1 + d)
            out_far_copy(r, d).wait_recv()
            half = mine.shape[0] // 2
            lo, hi = d * half, (d + 1) * half
            rest = slice(half, 2 * half) if d == 0 else slice(0, half)
            sum_near_out[r][d, lo:hi] = (mine[lo:hi] + sum_far_in[r][d].astype(jnp.float32)).astype(jnp.bfloat16)
            sum_near_out[r][d, rest] = mine[rest].astype(jnp.bfloat16)
            out_near_copy(r, d).start()

    def last(r):
        mine = pair(r, 3) + full[tp, slice(*GROUPS[r])].astype(jnp.float32).reshape(-1, WIDTH)
        for d in (0, 1):
            out_near_copy(r, d).wait_recv()
            mine = mine + sum_near_in[r][d].astype(jnp.float32)
        out[group_rows(r), :] = mine.astype(jnp.bfloat16)

    def attention(r):
        @pl.loop(*GROUPS[r])
        def _(s):
            for load in cache_loads(s):
                load.wait()
            append(s)
            slot(s, lengths[s], CACHE // BLOCK)

    attention(0)
    loads[3].wait()
    first(0)
    attention(1)
    far(0)
    first(1)
    attention(2)
    far(1)
    first(2)
    near(0)
    attention(3)
    far(2)
    first(3)
    near(1)
    last(0)
    far(3)
    near(2)
    last(1)
    near(3)
    last(2)
    last(3)
    for r in range(count):
        for i in range(4):
            sib_copy(r, i).wait_send()
        for d in (0, 1):
            out_far_copy(r, d).wait_send()
            out_near_copy(r, d).wait_send()
    for k in range(CHUNKS):
        for d in (0, 1):
            for hop in (1, 2, 3, 4):
                z_copy(k, hop, d, False).wait_send()
            far_copy(k, d).wait_send()
            near_copy(k, d).wait_send()
            y_copy(k, d, False).wait_send()
            half_copy(k, d, False).wait_send()
        for part in range(4):
            core_copy(k, part, False).wait_send()


def layer(order, lengths, kept, parents, hidden, gain, w_query, w_key, w_value, w_out, key_cache, value_cache):
    half = HEAD // 2
    freq = 500000.0 ** (-2.0 * np.arange(half, dtype=np.float64) / HEAD)
    freq = jnp.asarray(np.concatenate([freq, freq])[None].astype(np.float32))
    vmem = pl.BlockSpec(memory_space=pltpu.VMEM)
    hbm = pl.BlockSpec(memory_space=pltpu.HBM)
    nodes = SLOTS * NODES
    bf16, f32 = jnp.bfloat16, jnp.float32
    model = TP * WIDTH
    dma = pltpu.SemaphoreType.DMA
    sizes = [(hi - lo) * NODES for lo, hi in GROUPS]
    count = len(GROUPS)
    return pl.pallas_call(
        layer_kernel,
        out_shape=(
            jax.ShapeDtypeStruct((nodes, WIDTH), bf16),
            jax.ShapeDtypeStruct((SLOTS, 2, KEEP, HEAD), bf16),
        ),
        in_specs=[hbm] * 6 + [vmem] + [hbm] * 6,
        out_specs=(vmem, vmem),
        scratch_shapes=[
            pltpu.SMEM(order.shape, jnp.int32),
            pltpu.SMEM(lengths.shape, jnp.int32),
            pltpu.SMEM(kept.shape, jnp.int32),
            pltpu.VMEM(parents.shape, jnp.int32),
            pltpu.VMEM(freq.shape, f32),
            pltpu.VMEM((TP, SLOTS, NODES, WIDTH), bf16),
            pltpu.VMEM((SLOTS, NODES, NODES), f32),
            pltpu.VMEM((SLOTS, NODES, HEAD), f32),
            pltpu.VMEM((SLOTS, NODES, HEAD), f32),
            pltpu.VMEM((nodes, model), bf16),
            pltpu.VMEM((model, WIDTH), bf16),
            pltpu.VMEM((model, HEAD), bf16),
            pltpu.VMEM((model, HEAD), bf16),
            pltpu.VMEM((WIDTH, model), bf16),
            pltpu.VMEM((SLOTS, CACHE, HEAD), bf16),
            pltpu.VMEM((SLOTS, CACHE, HEAD), bf16),
            pltpu.VMEM((SLOTS, 3 * NODES, HEAD), bf16),
            pltpu.VMEM((SLOTS, NODES, HEAD), bf16),
            pltpu.VMEM((SLOTS, NODES, HEAD), bf16),
            pltpu.VMEM((CACHE // BLOCK, 3 * NODES, BLOCK), f32),
            pltpu.VMEM((nodes, WIDTH), bf16),
            pltpu.VMEM((2, SLOTS // 2, NODES, WIDTH), bf16),
            pltpu.VMEM((2, SLOTS // 2, NODES, WIDTH), bf16),
            pltpu.VMEM((2, SLOTS, NODES, WIDTH), bf16),
            pltpu.VMEM((2, SLOTS, NODES, WIDTH), bf16),
            dma((CHUNKS,)), dma((5,)),
            dma((2, 4, CHUNKS)), dma((2, 4, CHUNKS)),
            *[dma((2, CHUNKS))] * 8,
            dma((4, CHUNKS)), dma((4, CHUNKS)),
            dma((4,)), dma((2, SLOTS)),
            dma((count, 4)), dma((count, 4)),
            *[dma((count, 2))] * 4,
            *[pltpu.VMEM((NZ * SLOTS, size, WIDTH), bf16) for size in SIZES],
            *[pltpu.VMEM((4, n, WIDTH), bf16) for n in sizes] * 2,
            *[pltpu.VMEM((4, n, WIDTH), f32) for n in sizes],
            *[pltpu.VMEM((2, n // 2, WIDTH), bf16) for n in sizes] * 2,
            *[pltpu.VMEM((2, n, WIDTH), bf16) for n in sizes] * 2,
        ],
        compiler_params=pltpu.CompilerParams(
            collective_id=0, has_side_effects=True, vmem_limit_bytes=60 * 2**20
        ),
        name="layer",
    )(order, lengths, kept, parents, freq, hidden, gain, w_query, w_key, w_value, w_out, key_cache, value_cache)


def body(hidden_in, request_order, norm_gain, w_query, key_weight, value_weight, w_out,
         key_cache, cached_values, cache_lengths, tree_parent, kept_nodes):
    layer_out, appended = layer(
        request_order, cache_lengths, kept_nodes, tree_parent, hidden_in, norm_gain.reshape(1, -1), w_query, key_weight,
        value_weight, w_out, key_cache.reshape(SLOTS, CACHE, HEAD), cached_values.reshape(SLOTS, CACHE, HEAD),
    )
    return layer_out.reshape(SLOTS, NODES, WIDTH), appended.reshape(SLOTS, 2, KEEP, 1, HEAD)


def solution(mesh):
    placed = (
        P("req", None, "tp"), P(), P(), P(None, "tp"), P(None, "tp"), P(None, "tp"), P("tp", None),
        P("req", "tp", None, None), P("req", "tp", None, None), P("req"), P("req", None), P("req", None),
    )
    return jax.shard_map(
        body,
        mesh=mesh,
        in_specs=placed,
        out_specs=(P("req", None, "tp"), P("req", None, None, "tp", None)),
        check_vma=False,
    )
```
